32 devices in a mesh: dp: 8 (over z, y), expert: 4 (over x, core).
Axes of the slice: x: 2, y: 2, z: 4, core: 2. Of those that a mesh axis runs over, the one named last changes fastest.
Arguments:
- tokens: bfloat16 [4096, 2048], P(('dp', 'expert')), may hold values from -6 to 6
- cotangent: bfloat16 [4096, 2048], P(('dp', 'expert')), may hold values from -6 to 6
- lengths: int32 [4], replicated, may hold values from 512 to 1024, as said below
- piece_order: int32 [4, 8], replicated, may hold values from 0 to 7, each once within a row
- routes: int32 [4096, 8], P(('dp', 'expert')), may hold values from 0 to 15, all different within a row; in each aligned block of 128 rows (0 to 127, 128 to 255, ...) at most 96 rows name the same one
- attn_gain: float32 [2048], P(('dp', 'expert')), may hold values from 0.5 to 1.5
- w_query: float32 [2048, 2048], P(('dp', 'expert')), may hold values from -0.125 to 0.125
- w_key: float32 [2048, 2048], P(('dp', 'expert')), may hold values from -0.125 to 0.125
- w_value: float32 [2048, 2048], P(('dp', 'expert')), may hold values from -0.125 to 0.125
- w_output: float32 [2048, 2048], P(('dp', 'expert')), may hold values from -3 to 3
- query_gain: float32 [128], P(('dp', 'expert')), may hold values from 0.5 to 1.5
- key_gain: float32 [128], P(('dp', 'expert')), may hold values from 0.5 to 1.5
- moe_gain: float32 [2048], P(('dp', 'expert')), may hold values from 0.5 to 1.5
- w_router: float32 [2048, 16], P(('dp', 'expert')), may hold values from -0.0625 to 0.0625
- w_gate: float32 [16, 2048, 1024], P('expert', 'dp'), may hold values from -0.125 to 0.125
- w_up: float32 [16, 2048, 1024], P('expert', 'dp'), may hold values from -0.125 to 0.125
- w_down: float32 [16, 1024, 2048], P('expert', 'dp'), may hold values from -1 to 1
Outputs:
- block_out: bfloat16 [4096, 2048], P(('dp', 'expert'))
- grad_tokens: bfloat16 [4096, 2048], P(('dp', 'expert'))
- grad_attn_gain: float32 [2048], P(('dp', 'expert'))
- grad_query_w: float32 [2048, 2048], P(('dp', 'expert'))
- grad_key_w: float32 [2048, 2048], P(('dp', 'expert'))
- grad_value_w: float32 [2048, 2048], P(('dp', 'expert'))
- grad_output_w: float32 [2048, 2048], P(('dp', 'expert'))
- grad_query_gain: float32 [128], P(('dp', 'expert'))
- grad_key_gain: float32 [128], P(('dp', 'expert'))
- grad_moe_gain: float32 [2048], P(('dp', 'expert'))
- grad_router: float32 [2048, 16], P(('dp', 'expert'))
- grad_gate: float32 [16, 2048, 1024], P('expert', 'dp')
- grad_up: float32 [16, 2048, 1024], P('expert', 'dp')
- grad_down: float32 [16, 1024, 2048], P('expert', 'dp')
The draws below stay inside these ranges and needn't reach their ends.
Inputs may be any that keep to these rules, and one draw needn't show every extreme that they name: `lengths`: every length lies between 512 and 1024, and one sequence is 1024 long. `piece_order`: each row is a permutation of the 8 pieces. `routes`: each token names 8 different experts; among the rows of one device at most 96 name one expert, and some expert is named that often.
All inputs are finite; a program needn't handle non-finite values.
Results may differ from the reference program's by a relative error of at most 0.03.
Values may be sent and summed in bfloat16 or wider, within the bound.
No kernel may reach another device: no remote copies, remote signals or barrier semaphores. Data moves between devices by JAX's collectives and lax.ppermute only.
A program may use at most 384 MiB of HBM per device.

```python
import math
import jax
import jax.numpy as jnp
import numpy as np
from jax import lax

D = 2048
HEADS = 16
HD = 128
FF = 1024
TOP = 8
TOK_DEV = 128
EXPERTS = 16
CAP = 96
PIECES = 8
SEQS = 4
SEQ = 1024
TOKENS = 4096


def draw_lengths(key, part):
    first_key = jax.random.fold_in(key, 11)
    second_key = jax.random.fold_in(key, 23)
    drawn = jax.random.randint(first_key, (SEQS,), SEQ // 2, SEQ + 1)
    longest = jax.random.randint(second_key, (), 0, SEQS)
    return jnp.where(jnp.arange(SEQS) == longest, SEQ, drawn).astype(jnp.int32)


def block_scale(own_key, shape, pieces, smallest, top_value):
    factor_of, own = 1.0, jax.random.fold_in(own_key, 6)
    for dim, shards_of in pieces:
        steps = jnp.exp(jax.random.uniform(jax.random.fold_in(own, dim), (shards_of,), jnp.float32, smallest / len(pieces), top_value / len(pieces)))
        factor_of = factor_of * jnp.repeat(steps, shape[dim] // shards_of).reshape([-1 if axis == dim else 1 for axis in range(len(shape))])
    return factor_of


def shared_out(key, own, number, rows, count, top, bound, skew):
    sequence = jax.random.permutation(key, count)
    heavy_load, ordinary = shares(count, rows * top, bound, skew, True), shares(count, rows * top, bound, skew, False)
    places = jnp.arange(count)

    def named(sizes, rotation):
        used = int((sizes > 0).sum())
        fixed = max(1, used // 4)
        moved = fixed + (places - fixed + rotation * (used - fixed)) % max(1, count - fixed)
        return jnp.zeros((count,), jnp.int32).at[sequence[jnp.where(places < fixed, places, moved)]].set(jnp.asarray(sizes, jnp.int32))

    sizes = jnp.where(number % 4 == 0, named(heavy_load, number // 4), named(ordinary, number - number // 4 - 1))
    mixed = jax.random.permutation(jax.random.fold_in(own, 3), count)
    donor, sink = mixed[0:count // 2 * 2:2], mixed[1:count // 2 * 2:2]
    room = jnp.minimum(sizes[donor] - 1, bound - sizes[sink]) // 2
    room = jnp.where((donor == sequence[0]) | (sink == sequence[0]) | (sizes[sink] == 0), 0, jnp.maximum(room, 0))
    moved = jax.random.randint(jax.random.fold_in(own, 4), (count // 2,), 0, 1 << 20) % (room + 1)
    sizes = sizes.at[donor].add(-moved).at[sink].add(moved)
    labels = jnp.searchsorted(jnp.cumsum(sizes), jnp.arange(rows * top), side="right").astype(jnp.int32)
    grid = labels.reshape(top, rows).T
    grid = grid[jax.random.permutation(jax.random.fold_in(own, 1), rows)]
    rotation = jax.random.randint(jax.random.fold_in(own, 2), (rows, 1), 0, top)
    return jnp.take_along_axis(grid, (jnp.arange(top)[None, :] + rotation) % top, axis=1)


def shares(amount, total, reach, skew, full):
    loads = [(1 << 20) // math.isqrt(rank ** skew) + 1 for rank in range(1, amount + 1)]
    largest = reach if full else min(reach, max(-(-total // amount), total * loads[0] // sum(loads)))
    least = 1 if total - largest >= amount - 1 else 0
    given, spare = [largest] + [least] * (amount - 1), total - largest - least * (amount - 1)
    while spare > 0:
        free = [i for i in range(1, amount) if given[i] < largest] or [i for i in range(1, amount) if given[i] < reach]
        whole, left = sum([loads[i] for i in free]), spare
        for i in free:
            addition = min(reach - given[i], max(1, left * loads[i] // whole), spare)
            given[i] = given[i] + addition
            spare = spare - addition
    return np.array(given)


def normal_values(own_key, dims, spread, bound, shards=(), kind=jnp.bfloat16):
    array = spread * jax.random.normal(own_key, dims, jnp.float32)
    if shards:
        array = array * block_scale(own_key, dims, shards, -0.22, 0.18)
    return jnp.clip(array, -bound, bound).astype(kind)


def setup_inputs(seed: int = 0) -> dict:
    seeds = jax.random.split(jax.random.key(seed), 18)
    tokens = normal_values(seeds[0], (TOKENS, D), 1.0, 6.0, ((0, 32),))
    cotangent = normal_values(seeds[1], (TOKENS, D), 1.0, 6.0, ((0, 32),))
    lengths = draw_lengths(jax.random.fold_in(seeds[17], 71), 0)
    piece_order = jax.vmap(lambda own: jax.random.permutation(own, PIECES))(jax.random.split(seeds[3], SEQS)).reshape((SEQS, PIECES)).astype(jnp.int32)
    routes_keys = jax.random.split(jax.random.fold_in(seeds[4], 1), TOKENS // TOK_DEV)
    routes_turns = jax.random.permutation(jax.random.fold_in(seeds[4], 3), TOKENS // TOK_DEV)
    routes = jax.vmap(lambda own, number: shared_out(jax.random.fold_in(seeds[4], 2), own, number, TOK_DEV, EXPERTS, TOP, CAP, 2))(routes_keys, routes_turns).reshape((TOKENS, TOP))
    attn_gain = jnp.clip(1.0 + 0.1 * jax.random.normal(seeds[5], (D,), jnp.float32), 0.5, 1.5)
    w_query = normal_values(seeds[6], (D, D), D ** -0.5, 0.125, ((0, 32),), jnp.float32)
    w_key = normal_values(seeds[7], (D, D), D ** -0.5, 0.125, ((0, 32),), jnp.float32)
    w_value = normal_values(seeds[8], (D, D), D ** -0.5, 0.125, ((0, 32),), jnp.float32)
    w_output = normal_values(seeds[9], (D, D), (max(D // 512, 1)) ** -0.5, 3.0, ((0, 32),), jnp.float32)
    query_gain = jnp.clip(1.0 + 0.1 * jax.random.normal(seeds[10], (HD,), jnp.float32), 0.5, 1.5)
    key_gain = jnp.clip(1.0 + 0.1 * jax.random.normal(seeds[11], (HD,), jnp.float32), 0.5, 1.5)
    moe_gain = jnp.clip(1.0 + 0.1 * jax.random.normal(seeds[12], (D,), jnp.float32), 0.5, 1.5)
    w_router = normal_values(seeds[13], (D, EXPERTS), (4 * D) ** -0.5, 0.0625, ((0, 32),), jnp.float32)
    w_gate = normal_values(seeds[14], (EXPERTS, D, FF), D ** -0.5, 0.125, ((0, 4), (1, 8)), jnp.float32)
    w_up = normal_values(seeds[15], (EXPERTS, D, FF), D ** -0.5, 0.125, ((0, 4), (1, 8)), jnp.float32)
    w_down = normal_values(seeds[16], (EXPERTS, FF, D), (FF // 32) ** -0.5, 1.0, ((0, 4), (1, 8)), jnp.float32)
    return {"tokens": tokens, "cotangent": cotangent, "lengths": lengths, "piece_order": piece_order, "routes": routes, "attn_gain": attn_gain, "w_query": w_query, "w_key": w_key, "w_value": w_value, "w_output": w_output, "query_gain": query_gain, "key_gain": key_gain, "moe_gain": moe_gain, "w_router": w_router, "w_gate": w_gate, "w_up": w_up, "w_down": w_down}


norm_eps = 1e-06
rope_base = 10000.0
highest = lax.Precision.HIGHEST

@jax.custom_vjp
def low(v):
    return lax.optimization_barrier(v.astype(jnp.bfloat16)).astype(jnp.float32)

@jax.custom_vjp
def low_back(v):
    return v

def low_keep(v):
    return (low(v), None)

def low_pass(kept, grad):
    return (grad,)

def back_keep(v):
    return (v, None)

def back_low(kept, grad):
    return (low(grad),)
low.defvjp(low_keep, low_pass)
low_back.defvjp(back_keep, back_low)

def multiply(left_mat, right_mat):
    return jnp.dot(left_mat, right_mat, precision=highest, preferred_element_type=jnp.float32)

def rms_scale(features, gain_vec):
    return features * lax.rsqrt(lax.optimization_barrier(jnp.mean(features * features, axis=-1, keepdims=True)) + norm_eps) * gain_vec

def rotary(features, angles):
    half_dim = features.shape[-1] // 2
    cosine = jnp.cos(angles)[:, None, :]
    sine_part = jnp.sin(angles)[:, None, :]
    front_half = features[..., :half_dim]
    back_half = features[..., half_dim:]
    return jnp.concatenate([front_half * cosine - back_half * sine_part, back_half * cosine + front_half * sine_part], axis=-1)

def head_piece(angles, flat_vals, gain_vec):
    count = flat_vals.shape[0]
    shaped = flat_vals.reshape(count, HEADS, HD)
    return rotary(rms_scale(shaped, gain_vec), angles).reshape(count, HEADS * HD)

def expand_layout(values):
    trailing = values.shape[1:]
    shaped = values.reshape((PIECES, SEQS, TOK_DEV) + trailing)
    return jnp.swapaxes(shaped, 0, 1).reshape((SEQS, SEQ) + trailing)

def fold_layout(values):
    trailing = values.shape[2:]
    shaped = values.reshape((SEQS, PIECES, TOK_DEV) + trailing)
    return jnp.swapaxes(shaped, 0, 1).reshape((TOKENS,) + trailing)

def attend_sequence(packed):
    queries, keys_all, values_all, visible_keys = packed
    block_rows = min(512, SEQ)
    score_scale = 1.0 / HD ** 0.5

    def one_block(query_block):
        raw_scores = jnp.einsum('qhd,khd->hqk', query_block, keys_all, precision=highest) * score_scale
        raw_scores = low_back(raw_scores)
        masked = jnp.where(visible_keys[None, None, :], raw_scores, -jnp.inf)
        attn_probs = low(jax.nn.softmax(masked, axis=-1))
        return jnp.einsum('hqk,khd->qhd', attn_probs, values_all, precision=highest)
    query_blocks = queries.reshape(SEQ // block_rows, block_rows, HEADS, HD)
    return lax.map(jax.checkpoint(one_block), query_blocks).reshape(SEQ, HEADS, HD)

def expert_apply(packed):
    rows_in, gate_mat, up_mat, down_mat = packed
    rows_in = low_back(rows_in)
    gate_val = low_back(multiply(rows_in, low(gate_mat)))
    up_val = low_back(multiply(rows_in, low(up_mat)))
    inner_act = low(jax.nn.silu(gate_val) * up_val)
    return low_back(low(multiply(inner_act, low(down_mat))))

def reference(tokens, cotangent, lengths, piece_order, routes, attn_gain, w_query, w_key, w_value, w_output, query_gain, key_gain, moe_gain, w_router, w_gate, w_up, w_down):
    blocks = PIECES * SEQS
    offsets = jnp.arange(TOK_DEV, dtype=jnp.int32)
    piece_by_block = jnp.transpose(piece_order).reshape(-1)
    position = (piece_by_block[:, None] * TOK_DEV + offsets[None, :]).reshape(-1)
    half_dim = HD // 2
    frequency = rope_base ** (-(jnp.arange(half_dim, dtype=jnp.float32) * 2.0 / HD))
    angles = position.astype(jnp.float32)[:, None] * frequency[None, :]
    visible = expand_layout(position) < lengths[:, None]
    block_routes = routes.reshape(blocks, TOK_DEV * TOP)
    route_hot = (block_routes[:, :, None] == jnp.arange(EXPERTS, dtype=jnp.int32)).astype(jnp.int32)
    slot_rank = lax.optimization_barrier(jnp.sum((jnp.cumsum(route_hot, axis=1) - route_hot) * route_hot, axis=2))
    block_ids = jnp.broadcast_to(jnp.arange(blocks, dtype=jnp.int32)[:, None], block_routes.shape)
    token_ids = block_ids * TOK_DEV + jnp.arange(TOK_DEV * TOP, dtype=jnp.int32)[None, :] // TOP
    slot_table = jnp.zeros((EXPERTS, blocks, CAP), jnp.int32).at[block_routes, block_ids, slot_rank].set(token_ids + 1)
    slot_table = slot_table.reshape(EXPERTS, blocks * CAP)
    out_index = ((block_routes * blocks + block_ids) * CAP + slot_rank).reshape(-1)

    def forward(inputs, gain_one, wq, wk, wv, wo, gain_query, gain_key, gain_two, wr, wg, wu, wd):
        normed_one = low(rms_scale(inputs, gain_one))
        query_flat = low_back(multiply(normed_one, low(wq)))
        key_flat = low_back(multiply(normed_one, low(wk)))
        value_flat = low_back(low(multiply(normed_one, low(wv))))
        query_rot = low(head_piece(angles, query_flat, gain_query))
        key_rot = low(head_piece(angles, key_flat, gain_key))
        query_seq = expand_layout(query_rot.reshape(TOKENS, HEADS, HD))
        key_seq = expand_layout(key_rot.reshape(TOKENS, HEADS, HD))
        value_seq = expand_layout(value_flat.reshape(TOKENS, HEADS, HD))
        attended = lax.map(attend_sequence, (query_seq, key_seq, value_seq, visible))
        attended = low_back(low(fold_layout(attended).reshape(TOKENS, D)))
        hidden_one = inputs + low_back(multiply(attended, low(wo)))
        normed_two = low(rms_scale(hidden_one, gain_two))
        router_logits = low_back(multiply(normed_two, low(wr)))
        picked = jnp.take_along_axis(router_logits, routes, axis=1)
        gate_weights = jax.nn.softmax(picked, axis=-1)
        padded = jnp.concatenate([jnp.zeros((1, D), jnp.float32), normed_two], axis=0)
        expert_in = jnp.take(padded, slot_table, axis=0)
        produced = lax.map(jax.checkpoint(expert_apply), (expert_in, wg, wu, wd))
        gathered = jnp.take(produced.reshape(-1, D), out_index, axis=0).reshape(TOKENS, TOP, D)
        mixture = lax.optimization_barrier(jnp.sum(gate_weights[:, :, None] * gathered, axis=1))
        return hidden_one + mixture
    result, pullback = jax.vjp(forward, tokens.astype(jnp.float32), attn_gain, w_query, w_key, w_value, w_output, query_gain, key_gain, moe_gain, w_router, w_gate, w_up, w_down)
    all_grads = pullback(cotangent.astype(jnp.float32))
    return (result.astype(jnp.bfloat16), all_grads[0].astype(jnp.bfloat16), all_grads[1], all_grads[2], all_grads[3], all_grads[4], all_grads[5], all_grads[6], all_grads[7], all_grads[8], all_grads[9], all_grads[10], all_grads[11], all_grads[12])
```

```python
from functools import partial
import math

import jax
import jax.numpy as jnp
from jax import lax
from jax.sharding import PartitionSpec as P

HEADS = 16
HD = 128

norm_eps = 1e-06
rope_base = 10000.0
BF = jnp.bfloat16
F32 = jnp.float32


def rms_scale(features, gain_vec):
    return (
        features
        * lax.rsqrt(jnp.mean(features * features, axis=-1, keepdims=True) + norm_eps)
        * gain_vec
    )


def rotary(features, angles):
    half_dim = features.shape[-1] // 2
    cosine = jnp.cos(angles)[:, None, :]
    sine_part = jnp.sin(angles)[:, None, :]
    front_half = features[..., :half_dim]
    back_half = features[..., half_dim:]
    return jnp.concatenate(
        [front_half * cosine - back_half * sine_part, back_half * cosine + front_half * sine_part],
        axis=-1,
    )


def head_piece(angles, flat_vals, gain_vec):
    count = flat_vals.shape[0]
    shaped = flat_vals.reshape(count, -1, HD)
    return rotary(rms_scale(shaped, gain_vec), angles)


def dot(left_mat, right_mat):
    return jnp.dot(left_mat, right_mat, preferred_element_type=F32)


def dot_rows(left_mat, right_mat):
    return lax.dot_general(
        left_mat, right_mat, (((0,), (0,)), ((), ())), preferred_element_type=F32
    )


def dot_t(left_mat, right_mat):
    return lax.dot_general(
        left_mat, right_mat, (((1,), (1,)), ((), ())), preferred_element_type=F32
    )


BOTH = ("dp", "expert")


def swap(blocks, axes):
    return lax.all_to_all(blocks, axes, split_axis=0, concat_axis=0, tiled=True)


def gather(shard, axes):
    return lax.all_gather(shard, axes, axis=0, tiled=True)


def scatter(partial_sum, axes):
    return lax.psum_scatter(partial_sum, axes, scatter_dimension=0, tiled=True)


def on_device(
    tokens,
    cotangent,
    lengths,
    piece_order,
    routes,
    attn_gain,
    w_query,
    w_key,
    w_value,
    w_output,
    query_gain,
    key_gain,
    moe_gain,
    w_router,
    w_gate,
    w_up,
    w_down,
):
    rows, width = tokens.shape
    seq_id = lax.axis_index("expert")
    n_dp = lax.axis_size("dp")
    n_ex = lax.axis_size("expert")
    n_all = n_dp * n_ex
    local_count, _, ff = w_gate.shape
    expert_total = local_count * n_ex
    ff_part = ff // n_dp
    cols = width // n_dp
    wrows = w_query.shape[0]
    score_scale = 1.0 / math.sqrt(HD)

    gains = jnp.concatenate([attn_gain, moe_gain, query_gain, key_gain])
    gains_all = swap(jnp.broadcast_to(gains, (n_all, gains.shape[0])), BOTH)
    gw, hw = attn_gain.shape[0], query_gain.shape[0]
    gain_one = gains_all[:, :gw].reshape(-1)
    gain_two = gains_all[:, gw : 2 * gw].reshape(-1)
    gain_q = gains_all[:, 2 * gw : 2 * gw + hw].reshape(-1)
    gain_k = gains_all[:, 2 * gw + hw :].reshape(-1)

    seq_tokens = gather(tokens, "dp")
    qkv = jnp.stack([w_query, w_key, w_value]).astype(BF).reshape(3, wrows, n_dp, cols)
    qkv = swap(qkv.transpose(2, 1, 0, 3), "dp")
    qkv = gather(qkv.reshape(1, n_dp, wrows, 3 * cols), "expert")
    qkv = qkv.transpose(1, 0, 2, 3).reshape(width, 3 * cols)
    wo_all = gather(w_output.astype(BF), BOTH)
    wr_all = swap(
        jnp.broadcast_to(w_router.astype(BF).T, (n_all, expert_total, wrows)), BOTH
    )
    wr_all = wr_all.transpose(1, 0, 2).reshape(expert_total, width)
    w1 = jnp.stack([w_gate, w_up]).astype(BF).reshape(2, local_count, cols, n_dp, ff_part)
    w1 = swap(w1.transpose(3, 2, 0, 1, 4).reshape(n_dp, cols, -1), "dp").reshape(width, -1)
    w2 = w_down.astype(BF).reshape(local_count * ff_part, width)
    half = local_count * ff_part
    dy_all = gather(cotangent, BOTH)

    seq_in = seq_tokens.astype(F32)
    normed_one = rms_scale(seq_in, gain_one).astype(BF)
    qkv_flat = dot(normed_one, qkv)
    offsets = jnp.arange(rows, dtype=jnp.int32)
    position = (piece_order[seq_id][:, None] * rows + offsets[None, :]).reshape(-1)
    visible = position < lengths[seq_id]
    half_dim = HD // 2
    frequency = rope_base ** (-(jnp.arange(half_dim, dtype=F32) * 2.0 / HD))
    angles = position.astype(F32)[:, None] * frequency[None, :]
    query_rot, query_back = jax.vjp(partial(head_piece, angles), qkv_flat[:, :cols], gain_q)
    key_rot, key_back = jax.vjp(partial(head_piece, angles), qkv_flat[:, cols : 2 * cols], gain_k)
    query_bf = query_rot.astype(BF)
    key_bf = key_rot.astype(BF)
    value_bf = qkv_flat[:, 2 * cols :].astype(BF).reshape(-1, cols // HD, HD)
    scores = (
        jnp.einsum("qhd,khd->hqk", query_bf, key_bf, preferred_element_type=F32) * score_scale
    )
    scores = jnp.where(visible[None, None, :], scores, -jnp.inf)
    probs = jax.nn.softmax(scores, axis=-1)
    probs_bf = probs.astype(BF)
    attended = jnp.einsum("hqk,khd->qhd", probs_bf, value_bf, preferred_element_type=F32)
    attended = swap(attended.astype(BF).reshape(n_dp, rows, cols), "dp")
    attended = attended.transpose(1, 0, 2).reshape(rows, width)

    inputs = tokens.astype(F32)
    hidden_one = inputs + dot(attended, wo_all)
    normed_two = rms_scale(hidden_one, gain_two).astype(BF)
    router_logits = dot_t(normed_two, wr_all)
    expert_ids = jnp.arange(expert_total, dtype=jnp.int32)
    routed = jnp.any(routes[:, :, None] == expert_ids[None, None, :], axis=1)
    masked_logits = jnp.where(routed, router_logits, -jnp.inf)
    gates = jax.nn.softmax(masked_logits, axis=-1)
    gate_blocks = jnp.broadcast_to(
        gates.T.reshape(1, n_ex, local_count, rows), (n_dp, n_ex, local_count, rows)
    ).reshape(n_all, local_count, rows)
    my_gates = swap(gate_blocks, BOTH).transpose(0, 2, 1).reshape(n_all * rows, local_count)

    n2_all = gather(normed_two, BOTH)
    hidden_pre = dot(n2_all, w1)
    gate_val = hidden_pre[:, :half]
    up_val = hidden_pre[:, half:]
    wide_gates = jnp.repeat(my_gates, ff_part, axis=1)
    sig = jax.nn.sigmoid(gate_val)
    silu = gate_val * sig
    inner = (silu * up_val).astype(BF).astype(F32)
    gated_inner = (wide_gates * inner).astype(BF)
    back_inner = dot_t(dy_all, w2)
    gate_grads = jnp.sum(
        (inner * back_inner).reshape(-1, local_count, ff_part), axis=-1
    )
    inner_grad = wide_gates * back_inner
    pre_grad = jnp.concatenate(
        [inner_grad * up_val * sig * (1.0 + gate_val * (1.0 - sig)), inner_grad * silu], axis=1
    ).astype(BF)
    row_grads = dot_t(pre_grad, w1).astype(BF)
    token_grads = scatter(row_grads, BOTH).astype(F32)
    mixture = dot(gated_inner, w2).astype(BF)
    mixture, token_grads = lax.optimization_barrier((mixture, token_grads))
    mixed = scatter(mixture, BOTH).astype(F32)
    block_out = (hidden_one + mixed).astype(BF)
    down_grad = dot_rows(gated_inner, dy_all).reshape(local_count, ff_part, width)
    w1_grad = dot_rows(n2_all, pre_grad).astype(BF)
    w1_grad = swap(w1_grad.reshape(n_dp, cols, -1), "dp")
    w1_grad = (
        w1_grad.reshape(n_dp, cols, 2, local_count, ff_part)
        .transpose(2, 3, 1, 0, 4)
        .reshape(2, local_count, cols, ff)
        .astype(F32)
    )

    gg = swap(gate_grads.reshape(n_all, rows, local_count).transpose(0, 2, 1), BOTH)
    gg = gg.reshape(n_dp, n_ex, local_count, rows).sum(axis=0).reshape(expert_total, rows).T
    weighted = gates * gg
    logit_bf = (weighted - gates * jnp.sum(weighted, axis=-1, keepdims=True)).astype(BF)
    router_grad = dot_rows(normed_two, logit_bf)
    normed_two_grad = token_grads + dot(logit_bf, wr_all)
    _, norm_two_back = jax.vjp(rms_scale, hidden_one, gain_two)
    hidden_part, norm_two_grad = norm_two_back(normed_two_grad)
    hidden_grad = cotangent.astype(F32) + hidden_part
    attn_grad_bf = hidden_grad.astype(BF)
    output_grad = scatter(dot_rows(attended, attn_grad_bf).astype(BF), BOTH).astype(F32)
    attended_grad = dot_t(attn_grad_bf, wo_all).astype(BF)
    attended_grad = swap(attended_grad.reshape(rows, n_dp, cols).transpose(1, 0, 2), "dp")
    attended_grad = attended_grad.reshape(-1, cols // HD, HD)

    prob_grad = jnp.einsum("qhd,khd->hqk", attended_grad, value_bf, preferred_element_type=F32)
    score_grad = (
        probs * (prob_grad - jnp.sum(probs * prob_grad, axis=-1, keepdims=True))
    ).astype(BF)
    query_grad = (
        jnp.einsum("hqk,khd->qhd", score_grad, key_bf, preferred_element_type=F32) * score_scale
    )
    key_grad = (
        jnp.einsum("hqk,qhd->khd", score_grad, query_bf, preferred_element_type=F32) * score_scale
    )
    value_grad = jnp.einsum("hqk,qhd->khd", probs_bf, attended_grad, preferred_element_type=F32)
    query_flat_grad, query_gain_grad = query_back(query_grad)
    key_flat_grad, key_gain_grad = key_back(key_grad)
    qkv_grad = jnp.concatenate(
        [query_flat_grad.astype(BF), key_flat_grad.astype(BF), value_grad.reshape(-1, cols).astype(BF)],
        axis=1,
    )
    part_grad = dot_t(qkv_grad, qkv)
    seq_scale = lax.rsqrt(jnp.mean(seq_in * seq_in, axis=-1, keepdims=True) + norm_eps)
    norm_one_grad = jnp.sum(part_grad * (seq_in * seq_scale), axis=0)
    normed_one_grad = scatter(part_grad.astype(BF), "dp").astype(F32)
    _, norm_one_back = jax.vjp(lambda v: rms_scale(v, gain_one), inputs)
    (input_part,) = norm_one_back(normed_one_grad)
    grad_tokens = (hidden_grad + input_part).astype(BF)
    qkv_w = dot_rows(normed_one, qkv_grad).astype(BF)
    qkv_w = qkv_w.reshape(n_dp, n_ex, wrows, 3 * cols).transpose(1, 0, 2, 3)
    qkv_w = swap(qkv_w, "expert").astype(F32).sum(axis=0).astype(BF)
    qkv_w = swap(qkv_w, "dp").reshape(n_dp, wrows, 3, cols).transpose(2, 1, 0, 3)
    qkv_w = qkv_w.reshape(3, wrows, width).astype(F32)

    small = jnp.concatenate(
        [
            norm_one_grad.reshape(n_all, -1),
            norm_two_grad.reshape(n_all, -1),
            query_gain_grad.reshape(n_all, -1),
            key_gain_grad.reshape(n_all, -1),
            router_grad.reshape(n_all, -1),
        ],
        axis=1,
    )
    small = jnp.sum(swap(small, BOTH).reshape(n_all, -1), axis=0)
    return (
        block_out,
        grad_tokens,
        small[:gw],
        qkv_w[0],
        qkv_w[1],
        qkv_w[2],
        output_grad,
        small[2 * gw : 2 * gw + hw],
        small[2 * gw + hw : 2 * gw + 2 * hw],
        small[gw : 2 * gw],
        small[2 * gw + 2 * hw :].reshape(wrows, expert_total),
        w1_grad[0],
        w1_grad[1],
        down_grad,
    )


def solution(mesh):
    rows2 = P(("dp", "expert"), None)
    rows1 = P(("dp", "expert"))
    experts = P("expert", "dp", None)
    return jax.shard_map(
        on_device,
        mesh=mesh,
        in_specs=(rows2, rows2, P(), P(), rows2, rows1, rows2, rows2, rows2, rows2)
        + (rows1, rows1, rows1, rows2, experts, experts, experts),
        out_specs=(rows2, rows2, rows1, rows2, rows2, rows2, rows2)
        + (rows1, rows1, rows1, rows2, experts, experts, experts),
        check_vma=False,
    )
```

```python
from functools import partial
import math

import jax
import jax.numpy as jnp
from jax import lax
from jax.experimental import pallas as pl
from jax.sharding import PartitionSpec as P


HD = 128

norm_eps = 1e-06
rope_base = 10000.0
BF = jnp.bfloat16
F32 = jnp.float32


def rms_scale(features, gain_vec):
    return (
        features
        * lax.rsqrt(jnp.mean(features * features, axis=-1, keepdims=True) + norm_eps)
        * gain_vec
    )


def rotary(features, angles):
    half_dim = features.shape[-1] // 2
    cosine = jnp.cos(angles)[:, None, :]
    sine_part = jnp.sin(angles)[:, None, :]
    front_half = features[..., :half_dim]
    back_half = features[..., half_dim:]
    return jnp.concatenate(
        [front_half * cosine - back_half * sine_part, back_half * cosine + front_half * sine_part],
        axis=-1,
    )


def head_piece(angles, flat_vals, gain_vec):
    count = flat_vals.shape[0]
    shaped = flat_vals.reshape(count, -1, HD)
    return rotary(rms_scale(shaped, gain_vec), angles)


def dot(left_mat, right_mat):
    return jnp.dot(left_mat, right_mat, preferred_element_type=F32)


def dot_rows(left_mat, right_mat):
    return lax.dot_general(
        left_mat, right_mat, (((0,), (0,)), ((), ())), preferred_element_type=F32
    )


def dot_t(left_mat, right_mat):
    return lax.dot_general(
        left_mat, right_mat, (((1,), (1,)), ((), ())), preferred_element_type=F32
    )


BOTH = ("dp", "expert")


def swap(blocks, axes):
    return lax.all_to_all(blocks, axes, split_axis=0, concat_axis=0, tiled=True)


def gather(shard, axes):
    return lax.all_gather(shard, axes, axis=0, tiled=True)


def scatter(partial_sum, axes):
    return lax.psum_scatter(partial_sum, axes, scatter_dimension=0, tiled=True)


def ring_order(size):
    return list(range(0, size, 2)) + list(range(1, size, 2))[::-1]


def ring_perm(n_dp, steps):
    order = ring_order(n_dp // 2)
    size = len(order)
    pairs = []
    for spot in range(size):
        for inner in range(2):
            target = order[(spot + steps) % size]
            pairs.append((order[spot] * 2 + inner, target * 2 + inner))
    return pairs


def ring_shift(vals, steps):
    return lax.ppermute(vals, "dp", ring_perm(lax.axis_size("dp"), steps))


def flip(vals, axis, bit):
    size = lax.axis_size(axis)
    return lax.ppermute(vals, axis, [(i, i ^ bit) for i in range(size)])


def core_flip(vals):
    return flip(vals, "expert", 1)


def cross(vals, inner, bits):
    if inner == 0:
        return flip(vals, "expert", bits)
    if bits == 0:
        return flip(vals, "dp", 1)
    n_ex = lax.axis_size("expert")
    size = lax.axis_size("dp") * n_ex
    pairs = [(i, ((i // n_ex) ^ 1) * n_ex + ((i % n_ex) ^ bits)) for i in range(size)]
    return lax.ppermute(vals, BOTH, pairs)


def peers():
    size = lax.axis_size("expert")
    return [(inner, bits) for bits in range(0, size, 2) for inner in range(2)][1:]


def ring_blocks(vals):
    blocks = [vals]
    for _ in range(1, lax.axis_size("dp") // 2):
        blocks.append(ring_shift(blocks[-1], 1))
    return blocks


def add(left, right):
    return (left.astype(F32) + right.astype(F32)).astype(left.dtype)


def gather_peers(vals):
    return jnp.concatenate([vals] + [cross(vals, *peer) for peer in peers()], axis=0)


def reduce_peers(vals):
    total = vals[0].astype(F32)
    for spot, peer in enumerate(peers()):
        total = total + cross(vals[spot + 1], *peer).astype(F32)
    return total.astype(vals.dtype)


def walk_tables(n_dp):
    ring = ring_order(n_dp // 2)
    size = len(ring)
    ring_arr = jnp.array(ring, jnp.int32)
    spot_arr = jnp.array([ring.index(i) for i in range(size)], jnp.int32)
    member = lax.axis_index("dp")
    my_spot = spot_arr[member // 2]
    walk = jnp.arange(n_dp, dtype=jnp.int32)
    inner = (member % 2) ^ (walk % 2)
    source = ring_arr[(my_spot - walk // 2) % size] * 2 + inner
    target = ring_arr[(my_spot + walk // 2) % size] * 2 + inner
    step_of = ((my_spot - spot_arr[walk // 2]) % size) * 2 + inner
    return source, target, step_of


def walk_perm(n_dp, index):
    pairs = ring_perm(n_dp, index // 2)
    return [(src, dst ^ (index % 2)) for src, dst in pairs]


def walk_swap(blocks, tables):
    n_dp = blocks.shape[0]
    _, target, step_of = tables
    moved = []
    for index in range(n_dp):
        block = lax.dynamic_index_in_dim(blocks, target[index], 0, keepdims=False)
        if index:
            block = lax.ppermute(block, "dp", walk_perm(n_dp, index))
        moved.append(block)
    return jnp.take(jnp.stack(moved), step_of, axis=0)


def home(parts):
    total = parts[0].astype(F32)
    for step in range(1, len(parts)):
        total = total + ring_shift(parts[step], -step).astype(F32)
    return total


def expert_kernel(halves, width, xa, xb, ya, yb, w1, w1t, w2, w2t, pick, place, outs):
    ma, mb, ra, rb, pre_out, inner_out = outs
    step = pl.program_id(0)
    first = step < halves
    x_all = jnp.where(first, xa[...], xb[...])
    dy = jnp.where(first, ya[...], yb[...]).reshape(x_all.shape[0], width)
    x = x_all[:, :width]
    half = w2.shape[0]
    gates = dot(x_all[:, width:], pick[...])
    pre = dot(x, w1[...])
    gate_val, up_val = pre[:, :half], pre[:, half:]
    sig = 1.0 / (1.0 + jnp.exp(-gate_val))
    silu = gate_val * sig
    inner = (silu * up_val).astype(BF).astype(F32)
    gated = (gates * inner).astype(BF)
    inner_out[...] = gated
    mix = dot(gated, w2[...]).astype(BF)
    back = dot(dy, w2t[...])
    prod = inner * back
    prod_hi = prod.astype(BF)
    prod_lo = (prod - prod_hi.astype(F32)).astype(BF)
    gate_grad = (dot(prod_hi, place[...]) + dot(prod_lo, place[...])).astype(BF)
    inner_grad = gates * back
    gate_pre = (inner_grad * up_val * sig * (1.0 + gate_val * (1.0 - sig))).astype(BF)
    up_pre = (inner_grad * silu).astype(BF)
    pre_out[:, :half] = gate_pre
    pre_out[:, half:] = up_pre
    rows = (dot(gate_pre, w1t[:half, :]) + dot(up_pre, w1t[half:, :])).astype(BF)

    @pl.when(first)
    def _():
        ma[...] = mix
        ra[:, :width] = rows
        ra[:, width:] = gate_grad

    @pl.when(jnp.logical_not(first))
    def _():
        mb[...] = mix
        rb[:, :width] = rows
        rb[:, width:] = gate_grad


def experts(chunk, xa, xb, ya, yb, w1, w1t, w2, w2t, pick, place):
    count, wide = xa.shape
    rows, width = ya.shape[2:]
    half = w2.shape[0]
    tile = 2 * rows
    halves = count // tile
    front = lambda i: (jnp.minimum(i, halves - 1), 0)
    rear = lambda i: (jnp.maximum(i - halves, 0), 0)
    whole = lambda arr: pl.BlockSpec(arr.shape, lambda i: (0, 0), pipeline_mode=pl.Buffered(1))
    back_wide = width + place.shape[1]

    def body(xa, xb, ya, yb, w1, w1t, w2, w2t, pick, place, *outs):
        expert_kernel(halves, width, xa, xb, ya, yb, w1, w1t, w2, w2t, pick, place, outs)

    flops = 2 * 2 * count * width * half * 6
    return pl.pallas_call(
        body,
        grid=(2 * halves,),
        in_specs=[
            pl.BlockSpec((tile, wide), front),
            pl.BlockSpec((tile, wide), rear),
            pl.BlockSpec((2, None, rows, width), lambda i: (front(i)[0], chunk, 0, 0)),
            pl.BlockSpec((2, None, rows, width), lambda i: (rear(i)[0], chunk, 0, 0)),
        ]
        + [whole(arr) for arr in (w1, w1t, w2, w2t, pick, place)],
        out_specs=[
            pl.BlockSpec((tile, width), front),
            pl.BlockSpec((tile, width), rear),
            pl.BlockSpec((tile, back_wide), front),
            pl.BlockSpec((tile, back_wide), rear),
            pl.BlockSpec((tile, 2 * half), lambda i: (i, 0)),
            pl.BlockSpec((tile, half), lambda i: (i, 0)),
        ],
        out_shape=[
            jax.ShapeDtypeStruct((count, width), BF),
            jax.ShapeDtypeStruct((count, width), BF),
            jax.ShapeDtypeStruct((count, back_wide), BF),
            jax.ShapeDtypeStruct((count, back_wide), BF),
            jax.ShapeDtypeStruct((2 * count, 2 * half), BF),
            jax.ShapeDtypeStruct((2 * count, half), BF),
        ],
        cost_estimate=pl.CostEstimate(
            flops=flops, transcendentals=2 * count * half, bytes_accessed=20 * count * width
        ),
        name="experts",
    )(xa, xb, ya, yb, w1, w1t, w2, w2t, pick, place)


def lanes(count):
    return -(-count // 128) * 128


def on_device(
    tokens,
    cotangent,
    lengths,
    piece_order,
    routes,
    attn_gain,
    w_query,
    w_key,
    w_value,
    w_output,
    query_gain,
    key_gain,
    moe_gain,
    w_router,
    w_gate,
    w_up,
    w_down,
):
    rows, width = tokens.shape
    seq_id = lax.axis_index("expert")
    n_dp = lax.axis_size("dp")
    n_ex = lax.axis_size("expert")
    n_all = n_dp * n_ex
    local_count, _, ff = w_gate.shape
    expert_total = local_count * n_ex
    ff_part = ff // n_dp
    cols = width // n_dp
    wrows = w_query.shape[0]
    score_scale = 1.0 / math.sqrt(HD)

    gains = jnp.concatenate([attn_gain, moe_gain, query_gain, key_gain])
    gains_all = swap(jnp.broadcast_to(gains, (n_all, gains.shape[0])), BOTH)
    gw, hw = attn_gain.shape[0], query_gain.shape[0]
    gain_one = gains_all[:, :gw].reshape(-1)
    gain_two = gains_all[:, gw : 2 * gw].reshape(-1)
    gain_q = gains_all[:, 2 * gw : 2 * gw + hw].reshape(-1)
    gain_k = gains_all[:, 2 * gw + hw :].reshape(-1)

    seq_tokens = gather(tokens, "dp")
    member = lax.axis_index("dp")
    tables = walk_tables(n_dp)
    member_of_walk = tables[0]
    qkv = jnp.stack([w_query, w_key, w_value]).astype(BF).reshape(3, wrows, n_dp, cols)
    qkv = swap(qkv.transpose(2, 1, 0, 3), "dp")
    qkv = qkv.reshape(1, n_dp, wrows, 3 * cols)
    bit = 1
    while bit < n_ex:
        qkv = jnp.concatenate([qkv, flip(qkv, "expert", bit)], axis=0)
        bit *= 2
    qkv = jnp.take(qkv, seq_id ^ jnp.arange(n_ex, dtype=jnp.int32), axis=0)
    qkv = qkv.transpose(1, 0, 2, 3).reshape(width, 3 * cols)
    wo_all = gather(w_output.astype(BF), BOTH)
    wr_all = swap(
        jnp.broadcast_to(w_router.astype(BF).T, (n_all, expert_total, wrows)), BOTH
    )
    wr_all = wr_all.transpose(1, 0, 2).reshape(expert_total, width)
    w1 = jnp.stack([w_gate, w_up]).astype(BF).reshape(2, local_count, cols, n_dp, ff_part)
    w1 = w1.transpose(3, 2, 0, 1, 4).reshape(n_dp, cols, -1)
    w1 = walk_swap(w1, tables)
    w1 = w1.reshape(width, -1)
    w2 = w_down.astype(BF).reshape(local_count * ff_part, width)
    half = local_count * ff_part
    w1t, w2t = w1.T, w2.T
    dy_near = gather_peers(jnp.stack(ring_blocks(cotangent))[None])
    dy_far = core_flip(dy_near)

    seq_in = seq_tokens.astype(F32)
    normed_one = rms_scale(seq_in, gain_one).astype(BF)
    qkv_flat = dot(normed_one, qkv)
    offsets = jnp.arange(rows, dtype=jnp.int32)
    position = (piece_order[seq_id][:, None] * rows + offsets[None, :]).reshape(-1)
    visible = position < lengths[seq_id]
    half_dim = HD // 2
    frequency = rope_base ** (-(jnp.arange(half_dim, dtype=F32) * 2.0 / HD))
    angles = position.astype(F32)[:, None] * frequency[None, :]
    query_rot, query_back = jax.vjp(partial(head_piece, angles), qkv_flat[:, :cols], gain_q)
    key_rot, key_back = jax.vjp(partial(head_piece, angles), qkv_flat[:, cols : 2 * cols], gain_k)
    query_bf = query_rot.astype(BF)
    key_bf = key_rot.astype(BF)
    value_bf = qkv_flat[:, 2 * cols :].astype(BF).reshape(-1, cols // HD, HD)
    scores = (
        jnp.einsum("qhd,khd->hqk", query_bf, key_bf, preferred_element_type=F32) * score_scale
    )
    scores = jnp.where(visible[None, None, :], scores, -jnp.inf)
    probs = jax.nn.softmax(scores, axis=-1)
    probs_bf = probs.astype(BF)
    attended = jnp.einsum("hqk,khd->qhd", probs_bf, value_bf, preferred_element_type=F32)
    attended = swap(attended.astype(BF).reshape(n_dp, rows, cols), "dp")
    attended = attended.transpose(1, 0, 2).reshape(rows, width)

    inputs = tokens.astype(F32)
    hidden_one = inputs + dot(attended, wo_all)
    normed_two = rms_scale(hidden_one, gain_two).astype(BF)
    router_logits = dot_t(normed_two, wr_all)
    expert_ids = jnp.arange(expert_total, dtype=jnp.int32)
    routed = jnp.any(routes[:, :, None] == expert_ids[None, None, :], axis=1)
    masked_logits = jnp.where(routed, router_logits, -jnp.inf)
    gates = jax.nn.softmax(masked_logits, axis=-1)
    gates_hi = gates.astype(BF)
    gates_lo = (gates - gates_hi.astype(F32)).astype(BF)
    spare = lanes(2 * expert_total) - 2 * expert_total
    payload = jnp.concatenate(
        [normed_two, gates_hi, gates_lo, jnp.zeros((rows, spare), BF)], axis=1
    )
    unit = jnp.arange(half, dtype=jnp.int32) // ff_part + seq_id * local_count
    gate_col = jnp.arange(lanes(2 * expert_total), dtype=jnp.int32)
    pick = (
        (gate_col[:, None] == unit[None, :]) | (gate_col[:, None] == unit[None, :] + expert_total)
    ).astype(BF)
    grad_col = jnp.arange(lanes(expert_total * n_dp), dtype=jnp.int32)
    place = (grad_col[None, :] == (unit * n_dp + member)[:, None]).astype(BF)

    lean = n_all * rows > 4096
    n2_sets, mix_parts, home_parts, pre_grads, gated_inners = [], [], [], [], []
    w1_grad, down_grad = 0.0, 0.0
    near = None
    for step, block in enumerate(ring_blocks(payload)):
        if near is not None and not lean:
            block, near = lax.optimization_barrier((block, near))
        near = gather_peers(block)
        far = core_flip(near)
        ma, mb, ra, rb, pre_grad, gated_inner = experts(
            step, near, far, dy_near, dy_far, w1, w1t, w2, w2t, pick, place
        )
        part = add(ra, core_flip(rb)).reshape(-1, rows, ra.shape[1])
        home_parts.append(reduce_peers(part))
        if lean:
            mix_parts.append(reduce_peers(add(ma, core_flip(mb)).reshape(-1, rows, width)))
            cut = pre_grad.shape[0] // 2
            w1_grad = w1_grad + dot_rows(near[:, :width], pre_grad[:cut])
            w1_grad = w1_grad + dot_rows(far[:, :width], pre_grad[cut:])
            down_grad = down_grad + dot_rows(gated_inner[:cut], dy_near[:, step].reshape(-1, width))
            down_grad = down_grad + dot_rows(gated_inner[cut:], dy_far[:, step].reshape(-1, width))
            w1_grad, down_grad, dy_near, dy_far, mix_parts, home_parts, payload = (
                lax.optimization_barrier(
                    (w1_grad, down_grad, dy_near, dy_far, mix_parts, home_parts, payload)
                )
            )
        else:
            n2_sets += [near, far]
            mix_parts.append((ma, mb))
            pre_grads.append(pre_grad)
            gated_inners.append(gated_inner)
    returned = home(home_parts)
    token_grads = returned[:, :width]
    gg = returned[:, width : width + expert_total * n_dp].reshape(rows, expert_total, n_dp)
    gg = jnp.sum(gg, axis=-1)
    if not lean:
        mix_near = jnp.stack([m[0].reshape(-1, rows, width) for m in mix_parts], axis=1)
        mix_far = jnp.stack([m[1].reshape(-1, rows, width) for m in mix_parts], axis=1)
        mix_far, home_parts[-1] = lax.optimization_barrier((mix_far, home_parts[-1]))
        mix_near = add(mix_near, core_flip(mix_far))
        mix_parts = list(reduce_peers(mix_near))
        by_chunk = jnp.stack([g.reshape(2, -1, rows, half) for g in gated_inners], axis=2)
        by_chunk = by_chunk.reshape(2, -1, half)
        down_grad = dot_rows(by_chunk[0], dy_near.reshape(-1, width)) + dot_rows(
            by_chunk[1], dy_far.reshape(-1, width)
        )
        n2_all = jnp.concatenate([part[:, :width] for part in n2_sets], axis=0)
        w1_grad = dot_rows(n2_all, jnp.concatenate(pre_grads, axis=0))
    mixed = home(mix_parts)
    block_out = (hidden_one + mixed).astype(BF)
    down_grad = down_grad.reshape(local_count, ff_part, width)
    w1_grad = w1_grad.astype(BF)
    w1_grad = walk_swap(w1_grad.reshape(n_dp, cols, -1), tables)
    w1_grad = (
        w1_grad.reshape(n_dp, cols, 2, local_count, ff_part)
        .transpose(2, 3, 1, 0, 4)
        .reshape(2, local_count, cols, ff)
        .astype(F32)
    )
    weighted = gates * gg
    logit_bf = (weighted - gates * jnp.sum(weighted, axis=-1, keepdims=True)).astype(BF)
    router_grad = dot_rows(normed_two, logit_bf)
    normed_two_grad = token_grads + dot(logit_bf, wr_all)
    _, norm_two_back = jax.vjp(rms_scale, hidden_one, gain_two)
    hidden_part, norm_two_grad = norm_two_back(normed_two_grad)
    hidden_grad = cotangent.astype(F32) + hidden_part
    attn_grad_bf = hidden_grad.astype(BF)
    output_grad = scatter(dot_rows(attended, attn_grad_bf).astype(BF), BOTH).astype(F32)
    attended_grad = dot_t(attn_grad_bf, wo_all).astype(BF)
    attended_grad = swap(attended_grad.reshape(rows, n_dp, cols).transpose(1, 0, 2), "dp")
    attended_grad = attended_grad.reshape(-1, cols // HD, HD)

    prob_grad = jnp.einsum("qhd,khd->hqk", attended_grad, value_bf, preferred_element_type=F32)
    score_grad = (
        probs * (prob_grad - jnp.sum(probs * prob_grad, axis=-1, keepdims=True))
    ).astype(BF)
    query_grad = (
        jnp.einsum("hqk,khd->qhd", score_grad, key_bf, preferred_element_type=F32) * score_scale
    )
    key_grad = (
        jnp.einsum("hqk,qhd->khd", score_grad, query_bf, preferred_element_type=F32) * score_scale
    )
    value_grad = jnp.einsum("hqk,qhd->khd", probs_bf, attended_grad, preferred_element_type=F32)
    query_flat_grad, query_gain_grad = query_back(query_grad)
    key_flat_grad, key_gain_grad = key_back(key_grad)
    qkv_grad = jnp.concatenate(
        [query_flat_grad.astype(BF), key_flat_grad.astype(BF), value_grad.reshape(-1, cols).astype(BF)],
        axis=1,
    )
    walk_grad = jnp.take(qkv_grad.reshape(n_dp, rows, 3 * cols), member_of_walk, axis=0)
    part_grad = dot_t(walk_grad.reshape(-1, 3 * cols), qkv)
    walk_in = jnp.take(seq_tokens.reshape(n_dp, rows, width), member_of_walk, axis=0)
    seq_in = walk_in.reshape(-1, width).astype(F32)
    seq_scale = lax.rsqrt(jnp.mean(seq_in * seq_in, axis=-1, keepdims=True) + norm_eps)
    norm_one_grad = jnp.sum(part_grad * (seq_in * seq_scale), axis=0)
    part_bf = part_grad.astype(BF).reshape(n_dp // 2, 2, rows, width)
    sums = []
    for step in range(n_dp // 2):
        sums.append(add(part_bf[step, 0], flip(part_bf[step, 1], "dp", 1)))
    normed_one_grad = home(sums)
    _, norm_one_back = jax.vjp(lambda v: rms_scale(v, gain_one), inputs)
    (input_part,) = norm_one_back(normed_one_grad)
    grad_tokens = (hidden_grad + input_part).astype(BF)
    qkv_w = dot_rows(normed_one, qkv_grad).astype(BF)
    qkv_w = qkv_w.reshape(n_dp, n_ex, wrows, 3 * cols).transpose(1, 0, 2, 3)
    qkv_w = swap(qkv_w, "expert").astype(F32).sum(axis=0).astype(BF)
    qkv_w = swap(qkv_w, "dp").reshape(n_dp, wrows, 3, cols).transpose(2, 1, 0, 3)
    qkv_w = qkv_w.reshape(3, wrows, width).astype(F32)

    small = jnp.concatenate(
        [
            norm_one_grad.reshape(n_all, -1),
            norm_two_grad.reshape(n_all, -1),
            query_gain_grad.reshape(n_all, -1),
            key_gain_grad.reshape(n_all, -1),
            router_grad.reshape(n_all, -1),
        ],
        axis=1,
    )
    small = jnp.sum(swap(small, BOTH).reshape(n_all, -1), axis=0)
    return (
        block_out,
        grad_tokens,
        small[:gw],
        qkv_w[0],
        qkv_w[1],
        qkv_w[2],
        output_grad,
        small[2 * gw : 2 * gw + hw],
        small[2 * gw + hw : 2 * gw + 2 * hw],
        small[gw : 2 * gw],
        small[2 * gw + 2 * hw :].reshape(wrows, expert_total),
        w1_grad[0],
        w1_grad[1],
        down_grad,
    )


def solution(mesh):
    rows2 = P(("dp", "expert"), None)
    rows1 = P(("dp", "expert"))
    experts = P("expert", "dp", None)
    return jax.shard_map(
        on_device,
        mesh=mesh,
        in_specs=(rows2, rows2, P(), P(), rows2, rows1, rows2, rows2, rows2, rows2)
        + (rows1, rows1, rows1, rows2, experts, experts, experts),
        out_specs=(rows2, rows2, rows1, rows2, rows2, rows2, rows2)
        + (rows1, rows1, rows1, rows2, experts, experts, experts),
        check_vma=False,
    )
```

```python
from functools import partial
import math

import jax
import jax.numpy as jnp
from jax import lax
from jax.experimental import pallas as pl
from jax.experimental.pallas import tpu as pltpu
from jax.sharding import PartitionSpec as P


HD = 128

norm_eps = 1e-06
rope_base = 10000.0
BF = jnp.bfloat16
F32 = jnp.float32


def rms_scale(features, gain_vec):
    return (
        features
        * lax.rsqrt(jnp.mean(features * features, axis=-1, keepdims=True) + norm_eps)
        * gain_vec
    )


def rotary(features, angles):
    half_dim = features.shape[-1] // 2
    cosine = jnp.cos(angles)[:, None, :]
    sine_part = jnp.sin(angles)[:, None, :]
    front_half = features[..., :half_dim]
    back_half = features[..., half_dim:]
    return jnp.concatenate(
        [front_half * cosine - back_half * sine_part, back_half * cosine + front_half * sine_part],
        axis=-1,
    )


def head_piece(angles, flat_vals, gain_vec):
    count = flat_vals.shape[0]
    shaped = flat_vals.reshape(count, -1, HD)
    return rotary(rms_scale(shaped, gain_vec), angles)


def dot(left_mat, right_mat):
    return jnp.dot(left_mat, right_mat, preferred_element_type=F32)


def dot_rows(left_mat, right_mat):
    return lax.dot_general(
        left_mat, right_mat, (((0,), (0,)), ((), ())), preferred_element_type=F32
    )


def dot_t(left_mat, right_mat):
    return lax.dot_general(
        left_mat, right_mat, (((1,), (1,)), ((), ())), preferred_element_type=F32
    )


BOTH = ("dp", "expert")


def swap(blocks, axes):
    return lax.all_to_all(blocks, axes, split_axis=0, concat_axis=0, tiled=True)


def gather(shard, axes):
    return lax.all_gather(shard, axes, axis=0, tiled=True)


def scatter(partial_sum, axes):
    return lax.psum_scatter(partial_sum, axes, scatter_dimension=0, tiled=True)


def ring_order(size):
    return list(range(0, size, 2)) + list(range(1, size, 2))[::-1]


def ring_perm(n_dp, steps):
    order = ring_order(n_dp // 2)
    size = len(order)
    pairs = []
    for spot in range(size):
        for inner in range(2):
            target = order[(spot + steps) % size]
            pairs.append((order[spot] * 2 + inner, target * 2 + inner))
    return pairs


def ring_shift(vals, steps):
    return lax.ppermute(vals, "dp", ring_perm(lax.axis_size("dp"), steps))


def flip(vals, axis, bit):
    size = lax.axis_size(axis)
    return lax.ppermute(vals, axis, [(i, i ^ bit) for i in range(size)])


def core_flip(vals):
    return flip(vals, "expert", 1)


def cross(vals, inner, bits):
    if inner == 0:
        return flip(vals, "expert", bits)
    if bits == 0:
        return flip(vals, "dp", 1)
    n_ex = lax.axis_size("expert")
    size = lax.axis_size("dp") * n_ex
    pairs = [(i, ((i // n_ex) ^ 1) * n_ex + ((i % n_ex) ^ bits)) for i in range(size)]
    return lax.ppermute(vals, BOTH, pairs)


def peers():
    size = lax.axis_size("expert")
    return [(inner, bits) for bits in range(0, size, 2) for inner in range(2)][1:]


def ring_blocks(vals):
    blocks = [vals]
    for _ in range(1, lax.axis_size("dp") // 2):
        blocks.append(ring_shift(blocks[-1], 1))
    return blocks


def add(left, right):
    return (left.astype(F32) + right.astype(F32)).astype(left.dtype)


def gather_peers(vals):
    return jnp.concatenate([vals] + [cross(vals, *peer) for peer in peers()], axis=0)


def reduce_peers(vals):
    total = vals[0].astype(F32)
    for spot, peer in enumerate(peers()):
        total = total + cross(vals[spot + 1], *peer).astype(F32)
    return total.astype(vals.dtype)


def walk_tables(n_dp):
    ring = ring_order(n_dp // 2)
    size = len(ring)
    ring_arr = jnp.array(ring, jnp.int32)
    spot_arr = jnp.array([ring.index(i) for i in range(size)], jnp.int32)
    member = lax.axis_index("dp")
    my_spot = spot_arr[member // 2]
    walk = jnp.arange(n_dp, dtype=jnp.int32)
    inner = (member % 2) ^ (walk % 2)
    source = ring_arr[(my_spot - walk // 2) % size] * 2 + inner
    target = ring_arr[(my_spot + walk // 2) % size] * 2 + inner
    step_of = ((my_spot - spot_arr[walk // 2]) % size) * 2 + inner
    return source, target, step_of


def walk_perm(n_dp, index):
    pairs = ring_perm(n_dp, index // 2)
    return [(src, dst ^ (index % 2)) for src, dst in pairs]


def walk_swap(blocks, tables):
    n_dp = blocks.shape[0]
    _, target, step_of = tables
    moved = []
    for index in range(n_dp):
        block = lax.dynamic_index_in_dim(blocks, target[index], 0, keepdims=False)
        if index:
            block = lax.ppermute(block, "dp", walk_perm(n_dp, index))
        moved.append(block)
    return jnp.take(jnp.stack(moved), step_of, axis=0)


def home(parts):
    total = parts[0].astype(F32)
    for step in range(1, len(parts)):
        total = total + ring_shift(parts[step], -step).astype(F32)
    return total


def expert_kernel(halves, width, xa, xb, ya, yb, w1, w1t, w2, w2t, pick, place, outs):
    ma, mb, ra, rb, pre_out, inner_out = outs
    step = pl.program_id(0)
    first = step < halves
    x_all = jnp.where(first, xa[...], xb[...])
    dy = jnp.where(first, ya[...], yb[...]).reshape(x_all.shape[0], width)
    x = x_all[:, :width]
    half = w2.shape[0]
    gates = dot(x_all[:, width:], pick[...])
    pre = dot(x, w1[...])
    gate_val, up_val = pre[:, :half], pre[:, half:]
    sig = 1.0 / (1.0 + jnp.exp(-gate_val))
    silu = gate_val * sig
    inner = (silu * up_val).astype(BF).astype(F32)
    gated = (gates * inner).astype(BF)
    inner_out[...] = gated
    mix = dot(gated, w2[...]).astype(BF)
    back = dot(dy, w2t[...])
    prod = inner * back
    prod_hi = prod.astype(BF)
    prod_lo = (prod - prod_hi.astype(F32)).astype(BF)
    gate_grad = (dot(prod_hi, place[...]) + dot(prod_lo, place[...])).astype(BF)
    inner_grad = gates * back
    gate_pre = (inner_grad * up_val * sig * (1.0 + gate_val * (1.0 - sig))).astype(BF)
    up_pre = (inner_grad * silu).astype(BF)
    pre_out[:, :half] = gate_pre
    pre_out[:, half:] = up_pre
    rows = (dot(gate_pre, w1t[:half, :]) + dot(up_pre, w1t[half:, :])).astype(BF)

    @pl.when(first)
    def _():
        ma[...] = mix
        ra[:, :width] = rows
        ra[:, width:] = gate_grad

    @pl.when(jnp.logical_not(first))
    def _():
        mb[...] = mix
        rb[:, :width] = rows
        rb[:, width:] = gate_grad


def experts(chunk, xa, xb, ya, yb, w1, w1t, w2, w2t, pick, place):
    count, wide = xa.shape
    rows, width = ya.shape[2:]
    half = w2.shape[0]
    tile = 2 * rows
    halves = count // tile
    front = lambda i: (jnp.minimum(i, halves - 1), 0)
    rear = lambda i: (jnp.maximum(i - halves, 0), 0)
    whole = lambda arr: pl.BlockSpec(arr.shape, lambda i: (0, 0), pipeline_mode=pl.Buffered(1))
    back_wide = width + place.shape[1]

    def body(xa, xb, ya, yb, w1, w1t, w2, w2t, pick, place, *outs):
        expert_kernel(halves, width, xa, xb, ya, yb, w1, w1t, w2, w2t, pick, place, outs)

    flops = 2 * 2 * count * width * half * 6
    return pl.pallas_call(
        body,
        grid=(2 * halves,),
        in_specs=[
            pl.BlockSpec((tile, wide), front),
            pl.BlockSpec((tile, wide), rear),
            pl.BlockSpec((2, None, rows, width), lambda i: (front(i)[0], chunk, 0, 0)),
            pl.BlockSpec((2, None, rows, width), lambda i: (rear(i)[0], chunk, 0, 0)),
        ]
        + [whole(arr) for arr in (w1, w1t, w2, w2t, pick, place)],
        out_specs=[
            pl.BlockSpec((tile, width), front),
            pl.BlockSpec((tile, width), rear),
            pl.BlockSpec((tile, back_wide), front),
            pl.BlockSpec((tile, back_wide), rear),
            pl.BlockSpec((tile, 2 * half), lambda i: (i, 0)),
            pl.BlockSpec((tile, half), lambda i: (i, 0)),
        ],
        out_shape=[
            jax.ShapeDtypeStruct((count, width), BF),
            jax.ShapeDtypeStruct((count, width), BF),
            jax.ShapeDtypeStruct((count, back_wide), BF),
            jax.ShapeDtypeStruct((count, back_wide), BF),
            jax.ShapeDtypeStruct((2 * count, 2 * half), BF),
            jax.ShapeDtypeStruct((2 * count, half), BF),
        ],
        cost_estimate=pl.CostEstimate(
            flops=flops, transcendentals=2 * count * half, bytes_accessed=20 * count * width
        ),
        name="experts",
    )(xa, xb, ya, yb, w1, w1t, w2, w2t, pick, place)


def attend_kernel(scale, q, k, v, bias, out):
    scores = dot_t(q[...], k[...]) * scale + bias[...]
    weights = jnp.exp(scores - jnp.max(scores, axis=-1, keepdims=True))
    probs = (weights / jnp.sum(weights, axis=-1, keepdims=True)).astype(BF)
    out[...] = dot(probs, v[...]).astype(BF)


def attend(q, k, v, bias, scale):
    count, cols = q.shape
    tile = min(256, count)
    mine = pl.BlockSpec((tile, HD), lambda h, i: (i, h))
    full = pl.BlockSpec((count, HD), lambda h, i: (0, h))
    return pl.pallas_call(
        partial(attend_kernel, scale),
        grid=(cols // HD, count // tile),
        in_specs=[mine, full, full, pl.BlockSpec((1, count), lambda h, i: (0, 0))],
        out_specs=mine,
        out_shape=jax.ShapeDtypeStruct((count, cols), BF),
        cost_estimate=pl.CostEstimate(
            flops=4 * count * count * cols,
            transcendentals=count * count * cols // HD,
            bytes_accessed=8 * count * cols,
        ),
        name="attend",
    )(q, k, v, bias)


def attend_back_kernel(scale, q, k, v, bias, grad, dq, dk, dv, dk_sum, dv_sum):
    step = pl.program_id(1)
    scores = dot_t(q[...], k[...]) * scale + bias[...]
    weights = jnp.exp(scores - jnp.max(scores, axis=-1, keepdims=True))
    probs = weights / jnp.sum(weights, axis=-1, keepdims=True)
    prob_grad = dot_t(grad[...], v[...])
    mean = jnp.sum(probs * prob_grad, axis=-1, keepdims=True)
    score_grad = (probs * (prob_grad - mean)).astype(BF)
    dq[...] = dot(score_grad, k[...]) * scale
    dk_part = dot_rows(score_grad, q[...]) * scale
    dv_part = dot_rows(probs.astype(BF), grad[...])

    @pl.when(step == 0)
    def _():
        dk_sum[...] = dk_part
        dv_sum[...] = dv_part

    @pl.when(step > 0)
    def _():
        dk_sum[...] += dk_part
        dv_sum[...] += dv_part

    @pl.when(step == pl.num_programs(1) - 1)
    def _():
        dk[...] = dk_sum[...]
        dv[...] = dv_sum[...].astype(BF)


def attend_back(q, k, v, bias, grad, scale):
    count, cols = q.shape
    tile = min(256, count)
    mine = pl.BlockSpec((tile, HD), lambda h, i: (i, h))
    full = pl.BlockSpec((count, HD), lambda h, i: (0, h))
    return pl.pallas_call(
        partial(attend_back_kernel, scale),
        grid=(cols // HD, count // tile),
        in_specs=[mine, full, full, pl.BlockSpec((1, count), lambda h, i: (0, 0)), mine],
        out_specs=[mine, full, full],
        out_shape=[
            jax.ShapeDtypeStruct((count, cols), F32),
            jax.ShapeDtypeStruct((count, cols), F32),
            jax.ShapeDtypeStruct((count, cols), BF),
        ],
        scratch_shapes=[pltpu.VMEM((count, HD), F32), pltpu.VMEM((count, HD), F32)],
        cost_estimate=pl.CostEstimate(
            flops=10 * count * count * cols,
            transcendentals=count * count * cols // HD,
            bytes_accessed=20 * count * cols,
        ),
        name="attend_back",
    )(q, k, v, bias, grad)


def lanes(count):
    return -(-count // 128) * 128


def on_device(
    tokens,
    cotangent,
    lengths,
    piece_order,
    routes,
    attn_gain,
    w_query,
    w_key,
    w_value,
    w_output,
    query_gain,
    key_gain,
    moe_gain,
    w_router,
    w_gate,
    w_up,
    w_down,
):
    rows, width = tokens.shape
    seq_id = lax.axis_index("expert")
    n_dp = lax.axis_size("dp")
    n_ex = lax.axis_size("expert")
    n_all = n_dp * n_ex
    local_count, _, ff = w_gate.shape
    expert_total = local_count * n_ex
    ff_part = ff // n_dp
    cols = width // n_dp
    wrows = w_query.shape[0]
    score_scale = 1.0 / math.sqrt(HD)

    gains = jnp.concatenate([attn_gain, moe_gain, query_gain, key_gain])
    gains_all = swap(jnp.broadcast_to(gains, (n_all, gains.shape[0])), BOTH)
    gw, hw = attn_gain.shape[0], query_gain.shape[0]
    gain_one = gains_all[:, :gw].reshape(-1)
    gain_two = gains_all[:, gw : 2 * gw].reshape(-1)
    gain_q = gains_all[:, 2 * gw : 2 * gw + hw].reshape(-1)
    gain_k = gains_all[:, 2 * gw + hw :].reshape(-1)

    seq_tokens = gather(tokens, "dp")
    member = lax.axis_index("dp")
    tables = walk_tables(n_dp)
    member_of_walk = tables[0]
    qkv = jnp.stack([w_query, w_key, w_value]).astype(BF).reshape(3, wrows, n_dp, cols)
    qkv = swap(qkv.transpose(2, 1, 0, 3), "dp")
    qkv = qkv.reshape(1, n_dp, wrows, 3 * cols)
    bit = 1
    while bit < n_ex:
        qkv = jnp.concatenate([qkv, flip(qkv, "expert", bit)], axis=0)
        bit *= 2
    qkv = jnp.take(qkv, seq_id ^ jnp.arange(n_ex, dtype=jnp.int32), axis=0)
    qkv = qkv.transpose(1, 0, 2, 3).reshape(width, 3 * cols)
    wo_all = gather(w_output.astype(BF), BOTH)
    wr_all = swap(
        jnp.broadcast_to(w_router.astype(BF).T, (n_all, expert_total, wrows)), BOTH
    )
    wr_all = wr_all.transpose(1, 0, 2).reshape(expert_total, width)
    w1 = jnp.stack([w_gate, w_up]).astype(BF).reshape(2, local_count, cols, n_dp, ff_part)
    w1 = w1.transpose(3, 2, 0, 1, 4).reshape(n_dp, cols, -1)
    dy_ring = jnp.stack(ring_blocks(cotangent))[None]
    w1, dy_ring = lax.optimization_barrier((w1, dy_ring))
    w1 = walk_swap(w1, tables)
    w1 = w1.reshape(width, -1)
    w2 = w_down.astype(BF).reshape(local_count * ff_part, width)
    half = local_count * ff_part
    w1t, w2t = w1.T, w2.T
    dy_near = gather_peers(dy_ring)
    dy_far = core_flip(dy_near)

    seq_in = seq_tokens.astype(F32)
    normed_one = rms_scale(seq_in, gain_one).astype(BF)
    qkv_flat = dot(normed_one, qkv)
    offsets = jnp.arange(rows, dtype=jnp.int32)
    position = (piece_order[seq_id][:, None] * rows + offsets[None, :]).reshape(-1)
    visible = position < lengths[seq_id]
    half_dim = HD // 2
    frequency = rope_base ** (-(jnp.arange(half_dim, dtype=F32) * 2.0 / HD))
    angles = position.astype(F32)[:, None] * frequency[None, :]
    query_rot, query_back = jax.vjp(partial(head_piece, angles), qkv_flat[:, :cols], gain_q)
    key_rot, key_back = jax.vjp(partial(head_piece, angles), qkv_flat[:, cols : 2 * cols], gain_k)
    query_bf = query_rot.astype(BF).reshape(-1, cols)
    key_bf = key_rot.astype(BF).reshape(-1, cols)
    value_bf = qkv_flat[:, 2 * cols :].astype(BF)
    bias = jnp.where(visible, 0.0, -jnp.inf).astype(F32)[None, :]
    attended = attend(query_bf, key_bf, value_bf, bias, score_scale)
    attended = swap(attended.reshape(n_dp, rows, cols), "dp")
    attended = attended.transpose(1, 0, 2).reshape(rows, width)
    attended, w1, w1t, w2t = lax.optimization_barrier((attended, w1, w1t, w2t))

    inputs = tokens.astype(F32)
    hidden_one = inputs + dot(attended, wo_all)
    normed_two = rms_scale(hidden_one, gain_two).astype(BF)
    router_logits = dot_t(normed_two, wr_all)
    expert_ids = jnp.arange(expert_total, dtype=jnp.int32)
    routed = jnp.any(routes[:, :, None] == expert_ids[None, None, :], axis=1)
    masked_logits = jnp.where(routed, router_logits, -jnp.inf)
    gates = jax.nn.softmax(masked_logits, axis=-1)
    gates_hi = gates.astype(BF)
    gates_lo = (gates - gates_hi.astype(F32)).astype(BF)
    spare = lanes(2 * expert_total) - 2 * expert_total
    payload = jnp.concatenate(
        [normed_two, gates_hi, gates_lo, jnp.zeros((rows, spare), BF)], axis=1
    )
    unit = jnp.arange(half, dtype=jnp.int32) // ff_part + seq_id * local_count
    gate_col = jnp.arange(lanes(2 * expert_total), dtype=jnp.int32)
    pick = (
        (gate_col[:, None] == unit[None, :]) | (gate_col[:, None] == unit[None, :] + expert_total)
    ).astype(BF)
    grad_col = jnp.arange(lanes(expert_total * n_dp), dtype=jnp.int32)
    place = (grad_col[None, :] == (unit * n_dp + member)[:, None]).astype(BF)

    lean = n_all * rows > 4096
    n2_sets, mix_parts, home_parts, pre_grads, gated_inners = [], [], [], [], []
    w1_grad, down_grad = 0.0, 0.0
    near = None
    for step, block in enumerate(ring_blocks(payload)):
        if near is not None and not lean:
            block, near = lax.optimization_barrier((block, near))
        near = gather_peers(block)
        far = core_flip(near)
        ma, mb, ra, rb, pre_grad, gated_inner = experts(
            step, near, far, dy_near, dy_far, w1, w1t, w2, w2t, pick, place
        )
        part = add(ra, core_flip(rb)).reshape(-1, rows, ra.shape[1])
        home_parts.append(reduce_peers(part))
        if lean:
            mix_parts.append(reduce_peers(add(ma, core_flip(mb)).reshape(-1, rows, width)))
            cut = pre_grad.shape[0] // 2
            w1_grad = w1_grad + dot_rows(near[:, :width], pre_grad[:cut])
            w1_grad = w1_grad + dot_rows(far[:, :width], pre_grad[cut:])
            down_grad = down_grad + dot_rows(gated_inner[:cut], dy_near[:, step].reshape(-1, width))
            down_grad = down_grad + dot_rows(gated_inner[cut:], dy_far[:, step].reshape(-1, width))
            w1_grad, down_grad, dy_near, dy_far, mix_parts, home_parts, payload = (
                lax.optimization_barrier(
                    (w1_grad, down_grad, dy_near, dy_far, mix_parts, home_parts, payload)
                )
            )
        else:
            n2_sets += [near, far]
            mix_parts.append((ma, mb))
            pre_grads.append(pre_grad)
            gated_inners.append(gated_inner)
    returned = home(home_parts)
    if not lean:
        mix_near = jnp.stack([m[0].reshape(-1, rows, width) for m in mix_parts], axis=1)
        mix_far = jnp.stack([m[1].reshape(-1, rows, width) for m in mix_parts], axis=1)
        mix_far, returned = lax.optimization_barrier((mix_far, returned))
        mix_near = add(mix_near, core_flip(mix_far))
        mix_parts = list(reduce_peers(mix_near))
        by_chunk = jnp.stack([g.reshape(2, -1, rows, half) for g in gated_inners], axis=2)
        by_chunk = by_chunk.reshape(2, -1, half)
        down_grad = dot_rows(by_chunk[0], dy_near.reshape(-1, width)) + dot_rows(
            by_chunk[1], dy_far.reshape(-1, width)
        )
        n2_all = jnp.concatenate([part[:, :width] for part in n2_sets], axis=0)
        pre_all = jnp.concatenate(pre_grads, axis=0)
        w1_grad = dot_rows(n2_all, pre_all)
    w1_grad = w1_grad.astype(BF)
    w1_grad, returned = lax.optimization_barrier((w1_grad, returned))
    token_grads = returned[:, :width]
    gg = returned[:, width : width + expert_total * n_dp].reshape(rows, expert_total, n_dp)
    gg = jnp.sum(gg, axis=-1)
    mixed = home(mix_parts)
    down_grad = down_grad.reshape(local_count, ff_part, width)
    w1_grad = walk_swap(w1_grad.reshape(n_dp, cols, -1), tables)
    w1_grad = (
        w1_grad.reshape(n_dp, cols, 2, local_count, ff_part)
        .transpose(2, 3, 1, 0, 4)
        .reshape(2, local_count, cols, ff)
        .astype(F32)
    )
    weighted = gates * gg
    logit_bf = (weighted - gates * jnp.sum(weighted, axis=-1, keepdims=True)).astype(BF)
    router_grad = dot_rows(normed_two, logit_bf)
    normed_two_grad = token_grads + dot(logit_bf, wr_all)
    _, norm_two_back = jax.vjp(rms_scale, hidden_one, gain_two)
    hidden_part, norm_two_grad = norm_two_back(normed_two_grad)
    hidden_grad = cotangent.astype(F32) + hidden_part
    attn_grad_bf = hidden_grad.astype(BF)
    output_grad = scatter(dot_rows(attended, attn_grad_bf).astype(BF), BOTH).astype(F32)
    attended_grad = dot_t(attn_grad_bf, wo_all).astype(BF)
    attended_grad = swap(attended_grad.reshape(rows, n_dp, cols).transpose(1, 0, 2), "dp")
    attended_grad = attended_grad.reshape(-1, cols)

    query_grad, key_grad, value_grad = attend_back(
        query_bf, key_bf, value_bf, bias, attended_grad, score_scale
    )
    hidden_late, query_grad = lax.optimization_barrier((hidden_one, query_grad))
    block_out = (hidden_late + mixed).astype(BF)
    query_grad = query_grad.reshape(-1, cols // HD, HD)
    key_grad = key_grad.reshape(-1, cols // HD, HD)
    query_flat_grad, query_gain_grad = query_back(query_grad)
    key_flat_grad, key_gain_grad = key_back(key_grad)
    qkv_grad = jnp.concatenate(
        [query_flat_grad.astype(BF), key_flat_grad.astype(BF), value_grad],
        axis=1,
    )
    walk_grad = jnp.take(qkv_grad.reshape(n_dp, rows, 3 * cols), member_of_walk, axis=0)
    part_grad = dot_t(walk_grad.reshape(-1, 3 * cols), qkv)
    walk_in = jnp.take(seq_tokens.reshape(n_dp, rows, width), member_of_walk, axis=0)
    seq_in = walk_in.reshape(-1, width).astype(F32)
    seq_scale = lax.rsqrt(jnp.mean(seq_in * seq_in, axis=-1, keepdims=True) + norm_eps)
    norm_one_grad = jnp.sum(part_grad * (seq_in * seq_scale), axis=0)
    part_bf = part_grad.astype(BF).reshape(n_dp // 2, 2, rows, width)
    sums = []
    for step in range(n_dp // 2):
        sums.append(add(part_bf[step, 0], flip(part_bf[step, 1], "dp", 1)))
    normed_one_grad = home(sums)
    _, norm_one_back = jax.vjp(lambda v: rms_scale(v, gain_one), inputs)
    (input_part,) = norm_one_back(normed_one_grad)
    grad_tokens = (hidden_grad + input_part).astype(BF)
    qkv_w = dot_rows(normed_one, qkv_grad).astype(BF)
    qkv_w = qkv_w.reshape(n_dp, n_ex, wrows, 3 * cols).transpose(1, 0, 2, 3)
    qkv_w = swap(qkv_w, "expert").astype(F32).sum(axis=0).astype(BF)
    qkv_w = swap(qkv_w, "dp").reshape(n_dp, wrows, 3, cols).transpose(2, 1, 0, 3)
    qkv_w = qkv_w.reshape(3, wrows, width).astype(F32)

    small = jnp.concatenate(
        [
            norm_one_grad.reshape(n_all, -1),
            norm_two_grad.reshape(n_all, -1),
            query_gain_grad.reshape(n_all, -1),
            key_gain_grad.reshape(n_all, -1),
            router_grad.reshape(n_all, -1),
        ],
        axis=1,
    )
    small = jnp.sum(swap(small, BOTH).reshape(n_all, -1), axis=0)
    return (
        block_out,
        grad_tokens,
        small[:gw],
        qkv_w[0],
        qkv_w[1],
        qkv_w[2],
        output_grad,
        small[2 * gw : 2 * gw + hw],
        small[2 * gw + hw : 2 * gw + 2 * hw],
        small[gw : 2 * gw],
        small[2 * gw + 2 * hw :].reshape(wrows, expert_total),
        w1_grad[0],
        w1_grad[1],
        down_grad,
    )


def solution(mesh):
    rows2 = P(("dp", "expert"), None)
    rows1 = P(("dp", "expert"))
    experts = P("expert", "dp", None)
    return jax.shard_map(
        on_device,
        mesh=mesh,
        in_specs=(rows2, rows2, P(), P(), rows2, rows1, rows2, rows2, rows2, rows2)
        + (rows1, rows1, rows1, rows2, experts, experts, experts),
        out_specs=(rows2, rows2, rows1, rows2, rows2, rows2, rows2)
        + (rows1, rows1, rows1, rows2, experts, experts, experts),
        check_vma=False,
    )
```

```python
from functools import partial
import math

import jax
import jax.numpy as jnp
from jax import lax
from jax.experimental import pallas as pl
from jax.experimental.pallas import tpu as pltpu
from jax.sharding import PartitionSpec as P


HD = 128

norm_eps = 1e-06
rope_base = 10000.0
BF = jnp.bfloat16
F32 = jnp.float32


def rms_scale(features, gain_vec):
    return (
        features
        * lax.rsqrt(jnp.mean(features * features, axis=-1, keepdims=True) + norm_eps)
        * gain_vec
    )


def rotary(features, angles):
    half_dim = features.shape[-1] // 2
    cosine = jnp.cos(angles)[:, None, :]
    sine_part = jnp.sin(angles)[:, None, :]
    front_half = features[..., :half_dim]
    back_half = features[..., half_dim:]
    return jnp.concatenate(
        [front_half * cosine - back_half * sine_part, back_half * cosine + front_half * sine_part],
        axis=-1,
    )


def head_piece(angles, flat_vals, gain_vec):
    count = flat_vals.shape[0]
    shaped = flat_vals.reshape(count, -1, HD)
    return rotary(rms_scale(shaped, gain_vec), angles)


def dot(left_mat, right_mat):
    return jnp.dot(left_mat, right_mat, preferred_element_type=F32)


def dot_rows(left_mat, right_mat):
    return lax.dot_general(
        left_mat, right_mat, (((0,), (0,)), ((), ())), preferred_element_type=F32
    )


def dot_t(left_mat, right_mat):
    return lax.dot_general(
        left_mat, right_mat, (((1,), (1,)), ((), ())), preferred_element_type=F32
    )


BOTH = ("dp", "expert")


def swap(blocks, axes):
    return lax.all_to_all(blocks, axes, split_axis=0, concat_axis=0, tiled=True)


def gather(shard, axes):
    return lax.all_gather(shard, axes, axis=0, tiled=True)


def scatter(partial_sum, axes):
    return lax.psum_scatter(partial_sum, axes, scatter_dimension=0, tiled=True)


def ring_order(size):
    return list(range(0, size, 2)) + list(range(1, size, 2))[::-1]


def ring_perm(n_dp, steps):
    order = ring_order(n_dp // 2)
    size = len(order)
    pairs = []
    for spot in range(size):
        for inner in range(2):
            target = order[(spot + steps) % size]
            pairs.append((order[spot] * 2 + inner, target * 2 + inner))
    return pairs


def ring_shift(vals, steps):
    return lax.ppermute(vals, "dp", ring_perm(lax.axis_size("dp"), steps))


def flip(vals, axis, bit):
    size = lax.axis_size(axis)
    return lax.ppermute(vals, axis, [(i, i ^ bit) for i in range(size)])


def core_flip(vals):
    return flip(vals, "expert", 1)


def cross(vals, inner, bits):
    if inner == 0:
        return flip(vals, "expert", bits)
    if bits == 0:
        return flip(vals, "dp", 1)
    n_ex = lax.axis_size("expert")
    size = lax.axis_size("dp") * n_ex
    pairs = [(i, ((i // n_ex) ^ 1) * n_ex + ((i % n_ex) ^ bits)) for i in range(size)]
    return lax.ppermute(vals, BOTH, pairs)


def peers():
    size = lax.axis_size("expert")
    return [(inner, bits) for bits in range(0, size, 2) for inner in range(2)][1:]


def ring_blocks(vals):
    blocks = [vals]
    for step in range(1, lax.axis_size("dp") // 2):
        blocks.append(ring_shift(vals, step))
    return blocks


def pick_rows(vals, index):
    return vals.at[index].get(mode="promise_in_bounds")


def add32(left, right):
    return left.astype(F32) + right.astype(F32)


def add(left, right):
    return (left.astype(F32) + right.astype(F32)).astype(left.dtype)


def x_flip(vals):
    return flip(vals, "expert", 2)


def y_flip(vals):
    return flip(vals, "dp", 1)


def split_at(width):
    return width // 256 * 128


def gather_peers(vals):
    if lax.axis_size("expert") != 4:
        return jnp.stack([vals] + [cross(vals, *peer) for peer in peers()])
    cut = split_at(vals.shape[-1])
    left, right = vals[..., :cut], vals[..., cut:]
    left_y, right_x = y_flip(left), x_flip(right)
    left_pair, right_pair = jnp.stack([left, left_y]), jnp.stack([right, right_x])
    left_far, right_far = x_flip(left_pair), y_flip(right_pair)
    return jnp.stack(
        [
            vals,
            jnp.concatenate([left_y, right_far[0]], axis=-1),
            jnp.concatenate([left_far[0], right_x], axis=-1),
            jnp.concatenate([left_far[1], right_far[1]], axis=-1),
        ]
    )


def reduce_peers(vals):
    if lax.axis_size("expert") == 4:
        cut = split_at(vals.shape[-1])
        own, at_y, at_x, at_xy = vals[0], vals[1], vals[2], vals[3]
        left = x_flip(jnp.stack([at_x[..., :cut], at_xy[..., :cut]]))
        right = y_flip(jnp.stack([at_y[..., cut:], at_xy[..., cut:]]))
        left_y = add(at_y[..., :cut], left[1])
        right_x = add(at_x[..., cut:], right[1])
        left_y, right_x = y_flip(left_y), x_flip(right_x)
        left = add(add32(own[..., :cut], left[0]), left_y).astype(vals.dtype)
        right = add(add32(own[..., cut:], right[0]), right_x).astype(vals.dtype)
        return jnp.concatenate([left, right], axis=-1)
    total = vals[0].astype(F32)
    for spot, peer in enumerate(peers()):
        total = total + cross(vals[spot + 1], *peer).astype(F32)
    return total.astype(vals.dtype)


def walk_tables(n_dp):
    ring = ring_order(n_dp // 2)
    size = len(ring)
    ring_arr = jnp.array(ring, jnp.int32)
    spot_arr = jnp.array([ring.index(i) for i in range(size)], jnp.int32)
    member = lax.axis_index("dp")
    my_spot = spot_arr[member // 2]
    walk = jnp.arange(n_dp, dtype=jnp.int32)
    inner = (member % 2) ^ (walk % 2)
    source = ring_arr[(my_spot - walk // 2) % size] * 2 + inner
    target = ring_arr[(my_spot + walk // 2) % size] * 2 + inner
    step_of = ((my_spot - spot_arr[walk // 2]) % size) * 2 + inner
    return source, target, step_of


def walk_perm(n_dp, index):
    pairs = ring_perm(n_dp, index // 2)
    return [(src, dst ^ (index % 2)) for src, dst in pairs]


def walk_swap(blocks, tables):
    n_dp = blocks.shape[0]
    _, target, step_of = tables
    moved = []
    for index in range(n_dp):
        block = lax.dynamic_index_in_dim(blocks, target[index], 0, keepdims=False)
        if index:
            block = lax.ppermute(block, "dp", walk_perm(n_dp, index))
        moved.append(block)
    return pick_rows(jnp.stack(moved), step_of)


def home(parts):
    total = parts[0].astype(F32)
    for step in range(1, len(parts)):
        total = total + ring_shift(parts[step], -step).astype(F32)
    return total


def expert_kernel(halves, width, xa, xb, ya, yb, w1, w1t, w2, w2t, pick, place, outs):
    ma, mb, ra, rb, pre_out, inner_out = outs
    step = pl.program_id(0)
    first = step < halves
    x_all = jnp.where(first, xa[...], xb[...])
    dy = jnp.where(first, ya[...], yb[...]).reshape(x_all.shape[0], width)
    x = x_all[:, :width]
    half = w2.shape[0]
    gates = dot(x_all[:, width:], pick[...])
    pre = dot(x, w1[...])
    gate_val, up_val = pre[:, :half], pre[:, half:]
    sig = 1.0 / (1.0 + jnp.exp(-gate_val))
    silu = gate_val * sig
    inner = (silu * up_val).astype(BF).astype(F32)
    gated = (gates * inner).astype(BF)
    inner_out[...] = gated
    mix = dot(gated, w2[...]).astype(BF)
    back = dot(dy, w2t[...])
    prod = inner * back
    prod_hi = prod.astype(BF)
    prod_lo = (prod - prod_hi.astype(F32)).astype(BF)
    gate_grad = (dot(prod_hi, place[...]) + dot(prod_lo, place[...])).astype(BF)
    inner_grad = gates * back
    gate_pre = (inner_grad * up_val * sig * (1.0 + gate_val * (1.0 - sig))).astype(BF)
    up_pre = (inner_grad * silu).astype(BF)
    pre_out[:, :half] = gate_pre
    pre_out[:, half:] = up_pre
    rows = (dot(gate_pre, w1t[:half, :]) + dot(up_pre, w1t[half:, :])).astype(BF)

    @pl.when(first)
    def _():
        ma[...] = mix
        ra[:, :width] = rows
        ra[:, width:] = gate_grad

    @pl.when(jnp.logical_not(first))
    def _():
        mb[...] = mix
        rb[:, :width] = rows
        rb[:, width:] = gate_grad


def experts(chunk, xa, xb, ya, yb, w1, w1t, w2, w2t, pick, place):
    count, wide = xa.shape
    rows, width = ya.shape[2:]
    half = w2.shape[0]
    tile = 2 * rows
    halves = count // tile
    front = lambda i: (jnp.minimum(i, halves - 1), 0)
    rear = lambda i: (jnp.maximum(i - halves, 0), 0)
    whole = lambda arr: pl.BlockSpec(arr.shape, lambda i: (0, 0), pipeline_mode=pl.Buffered(1))
    back_wide = width + place.shape[1]

    def body(xa, xb, ya, yb, w1, w1t, w2, w2t, pick, place, *outs):
        expert_kernel(halves, width, xa, xb, ya, yb, w1, w1t, w2, w2t, pick, place, outs)

    flops = 2 * 2 * count * width * half * 6
    return pl.pallas_call(
        body,
        grid=(2 * halves,),
        in_specs=[
            pl.BlockSpec((tile, wide), front),
            pl.BlockSpec((tile, wide), rear),
            pl.BlockSpec((2, None, rows, width), lambda i: (front(i)[0], chunk, 0, 0)),
            pl.BlockSpec((2, None, rows, width), lambda i: (rear(i)[0], chunk, 0, 0)),
        ]
        + [whole(arr) for arr in (w1, w1t, w2, w2t, pick, place)],
        out_specs=[
            pl.BlockSpec((tile, width), front),
            pl.BlockSpec((tile, width), rear),
            pl.BlockSpec((tile, back_wide), front),
            pl.BlockSpec((tile, back_wide), rear),
            pl.BlockSpec((tile, 2 * half), lambda i: (i, 0)),
            pl.BlockSpec((tile, half), lambda i: (i, 0)),
        ],
        out_shape=[
            jax.ShapeDtypeStruct((count, width), BF),
            jax.ShapeDtypeStruct((count, width), BF),
            jax.ShapeDtypeStruct((count, back_wide), BF),
            jax.ShapeDtypeStruct((count, back_wide), BF),
            jax.ShapeDtypeStruct((2 * count, 2 * half), BF),
            jax.ShapeDtypeStruct((2 * count, half), BF),
        ],
        cost_estimate=pl.CostEstimate(
            flops=flops, transcendentals=2 * count * half, bytes_accessed=20 * count * width
        ),
        name="experts",
    )(xa, xb, ya, yb, w1, w1t, w2, w2t, pick, place)


def attend_kernel(scale, q, k, v, bias, out):
    scores = dot_t(q[...], k[...]) * scale + bias[...]
    weights = jnp.exp(scores - jnp.max(scores, axis=-1, keepdims=True))
    probs = (weights / jnp.sum(weights, axis=-1, keepdims=True)).astype(BF)
    out[...] = dot(probs, v[...]).astype(BF)


def attend(q, k, v, bias, scale):
    count, cols = q.shape
    tile = min(256, count)
    mine = pl.BlockSpec((tile, HD), lambda h, i: (i, h))
    full = pl.BlockSpec((count, HD), lambda h, i: (0, h))
    return pl.pallas_call(
        partial(attend_kernel, scale),
        grid=(cols // HD, count // tile),
        in_specs=[mine, full, full, pl.BlockSpec((1, count), lambda h, i: (0, 0))],
        out_specs=mine,
        out_shape=jax.ShapeDtypeStruct((count, cols), BF),
        cost_estimate=pl.CostEstimate(
            flops=4 * count * count * cols,
            transcendentals=count * count * cols // HD,
            bytes_accessed=8 * count * cols,
        ),
        name="attend",
    )(q, k, v, bias)


def attend_back_kernel(scale, q, k, v, bias, grad, dq, dk, dv, dk_sum, dv_sum):
    step = pl.program_id(1)
    scores = dot_t(q[...], k[...]) * scale + bias[...]
    weights = jnp.exp(scores - jnp.max(scores, axis=-1, keepdims=True))
    probs = weights / jnp.sum(weights, axis=-1, keepdims=True)
    prob_grad = dot_t(grad[...], v[...])
    mean = jnp.sum(probs * prob_grad, axis=-1, keepdims=True)
    score_grad = (probs * (prob_grad - mean)).astype(BF)
    dq[...] = dot(score_grad, k[...]) * scale
    dk_part = dot_rows(score_grad, q[...]) * scale
    dv_part = dot_rows(probs.astype(BF), grad[...])

    @pl.when(step == 0)
    def _():
        dk_sum[...] = dk_part
        dv_sum[...] = dv_part

    @pl.when(step > 0)
    def _():
        dk_sum[...] += dk_part
        dv_sum[...] += dv_part

    @pl.when(step == pl.num_programs(1) - 1)
    def _():
        dk[...] = dk_sum[...]
        dv[...] = dv_sum[...].astype(BF)


def attend_back(q, k, v, bias, grad, scale):
    count, cols = q.shape
    tile = min(256, count)
    mine = pl.BlockSpec((tile, HD), lambda h, i: (i, h))
    full = pl.BlockSpec((count, HD), lambda h, i: (0, h))
    return pl.pallas_call(
        partial(attend_back_kernel, scale),
        grid=(cols // HD, count // tile),
        in_specs=[mine, full, full, pl.BlockSpec((1, count), lambda h, i: (0, 0)), mine],
        out_specs=[mine, full, full],
        out_shape=[
            jax.ShapeDtypeStruct((count, cols), F32),
            jax.ShapeDtypeStruct((count, cols), F32),
            jax.ShapeDtypeStruct((count, cols), BF),
        ],
        scratch_shapes=[pltpu.VMEM((count, HD), F32), pltpu.VMEM((count, HD), F32)],
        cost_estimate=pl.CostEstimate(
            flops=10 * count * count * cols,
            transcendentals=count * count * cols // HD,
            bytes_accessed=20 * count * cols,
        ),
        name="attend_back",
    )(q, k, v, bias, grad)


def lanes(count):
    return -(-count // 128) * 128


def on_device(
    tokens,
    cotangent,
    lengths,
    piece_order,
    routes,
    attn_gain,
    w_query,
    w_key,
    w_value,
    w_output,
    query_gain,
    key_gain,
    moe_gain,
    w_router,
    w_gate,
    w_up,
    w_down,
):
    rows, width = tokens.shape
    seq_id = lax.axis_index("expert")
    n_dp = lax.axis_size("dp")
    n_ex = lax.axis_size("expert")
    n_all = n_dp * n_ex
    local_count, _, ff = w_gate.shape
    expert_total = local_count * n_ex
    ff_part = ff // n_dp
    cols = width // n_dp
    wrows = w_query.shape[0]
    score_scale = 1.0 / math.sqrt(HD)

    gains = jnp.concatenate(
        [attn_gain, moe_gain, query_gain, key_gain, w_router.T.reshape(-1)]
    )
    gains_all = swap(jnp.broadcast_to(gains, (n_all, gains.shape[0])), BOTH)
    gw, hw = attn_gain.shape[0], query_gain.shape[0]
    gain_one = gains_all[:, :gw].reshape(-1)
    gain_two = gains_all[:, gw : 2 * gw].reshape(-1)
    gain_q = gains_all[:, 2 * gw : 2 * gw + hw].reshape(-1)
    gain_k = gains_all[:, 2 * gw + hw : 2 * gw + 2 * hw].reshape(-1)
    wr_all = gains_all[:, 2 * gw + 2 * hw :].reshape(n_all, expert_total, wrows)
    wr_all = wr_all.transpose(1, 0, 2).reshape(expert_total, width).astype(BF)

    seq_tokens = gather(tokens, "dp")
    member = lax.axis_index("dp")
    tables = walk_tables(n_dp)
    member_of_walk = tables[0]
    qkv = jnp.stack([w_query, w_key, w_value]).astype(BF).reshape(3, wrows, n_dp, cols)
    qkv = swap(qkv.transpose(2, 1, 0, 3), "dp")
    qkv = qkv.reshape(1, n_dp, wrows, 3 * cols)
    bit = 1
    while bit < n_ex:
        qkv = jnp.concatenate([qkv, flip(qkv, "expert", bit)], axis=0)
        bit *= 2
    qkv = pick_rows(qkv, seq_id ^ jnp.arange(n_ex, dtype=jnp.int32))
    qkv = qkv.transpose(1, 0, 2, 3).reshape(width, 3 * cols)
    wo_all = gather(w_output.astype(BF), BOTH)
    w1 = jnp.stack([w_gate, w_up]).astype(BF).reshape(2, local_count, cols, n_dp, ff_part)
    w1 = w1.transpose(3, 2, 0, 1, 4).reshape(n_dp, cols, -1)
    dy_ring = jnp.stack(ring_blocks(cotangent))
    w1 = walk_swap(w1, tables)
    w1 = w1.reshape(width, -1)
    w2 = w_down.astype(BF).reshape(local_count * ff_part, width)
    half = local_count * ff_part
    w1t, w2t = w1.T, w2.T
    dy_near = gather_peers(dy_ring)
    dy_far = core_flip(dy_near)

    seq_in = seq_tokens.astype(F32)
    normed_one = rms_scale(seq_in, gain_one).astype(BF)
    qkv_flat = dot(normed_one, qkv)
    offsets = jnp.arange(rows, dtype=jnp.int32)
    position = (piece_order[seq_id][:, None] * rows + offsets[None, :]).reshape(-1)
    visible = position < lengths[seq_id]
    half_dim = HD // 2
    frequency = rope_base ** (-(jnp.arange(half_dim, dtype=F32) * 2.0 / HD))
    angles = position.astype(F32)[:, None] * frequency[None, :]
    query_rot, query_back = jax.vjp(partial(head_piece, angles), qkv_flat[:, :cols], gain_q)
    key_rot, key_back = jax.vjp(partial(head_piece, angles), qkv_flat[:, cols : 2 * cols], gain_k)
    query_bf = query_rot.astype(BF).reshape(-1, cols)
    key_bf = key_rot.astype(BF).reshape(-1, cols)
    value_bf = qkv_flat[:, 2 * cols :].astype(BF)
    bias = jnp.where(visible, 0.0, -jnp.inf).astype(F32)[None, :]
    attended = attend(query_bf, key_bf, value_bf, bias, score_scale)
    attended = swap(attended.reshape(n_dp, rows, cols), "dp")
    attended = attended.transpose(1, 0, 2).reshape(rows, width)
    attended, w1, w1t, w2t = lax.optimization_barrier((attended, w1, w1t, w2t))

    inputs = tokens.astype(F32)
    hidden_one = inputs + dot(attended, wo_all)
    normed_two = rms_scale(hidden_one, gain_two).astype(BF)
    router_logits = dot_t(normed_two, wr_all)
    expert_ids = jnp.arange(expert_total, dtype=jnp.int32)
    routed = jnp.any(routes[:, :, None] == expert_ids[None, None, :], axis=1)
    masked_logits = jnp.where(routed, router_logits, -jnp.inf)
    gates = jax.nn.softmax(masked_logits, axis=-1)
    gates_hi = gates.astype(BF)
    gates_lo = (gates - gates_hi.astype(F32)).astype(BF)
    spare = lanes(2 * expert_total) - 2 * expert_total
    payload = jnp.concatenate(
        [normed_two, gates_hi, gates_lo, jnp.zeros((rows, spare), BF)], axis=1
    )
    unit = jnp.arange(half, dtype=jnp.int32) // ff_part + seq_id * local_count
    gate_col = jnp.arange(lanes(2 * expert_total), dtype=jnp.int32)
    pick = (
        (gate_col[:, None] == unit[None, :]) | (gate_col[:, None] == unit[None, :] + expert_total)
    ).astype(BF)
    grad_col = jnp.arange(lanes(expert_total * n_dp), dtype=jnp.int32)
    place = (grad_col[None, :] == (unit * n_dp + member)[:, None]).astype(BF)

    lean = n_all * rows > 4096
    n2_sets, mix_parts, home_parts, pre_grads, gated_inners = [], [], [], [], []
    w1_grad, down_grad = 0.0, 0.0
    for step, block in enumerate(ring_blocks(payload)):
        near = gather_peers(block).reshape(-1, block.shape[-1])
        far = core_flip(near)
        ma, mb, ra, rb, pre_grad, gated_inner = experts(
            step, near, far, dy_near, dy_far, w1, w1t, w2, w2t, pick, place
        )
        part = add(ra, core_flip(rb)).reshape(-1, rows, ra.shape[1])
        home_parts.append(reduce_peers(part))
        if lean:
            mix_parts.append(reduce_peers(add(ma, core_flip(mb)).reshape(-1, rows, width)))
            cut = pre_grad.shape[0] // 2
            w1_grad = w1_grad + dot_rows(near[:, :width], pre_grad[:cut])
            w1_grad = w1_grad + dot_rows(far[:, :width], pre_grad[cut:])
            down_grad = down_grad + dot_rows(gated_inner[:cut], dy_near[:, step].reshape(-1, width))
            down_grad = down_grad + dot_rows(gated_inner[cut:], dy_far[:, step].reshape(-1, width))
            w1_grad, down_grad, dy_near, dy_far, mix_parts, home_parts, payload = (
                lax.optimization_barrier(
                    (w1_grad, down_grad, dy_near, dy_far, mix_parts, home_parts, payload)
                )
            )
        else:
            n2_sets += [near, far]
            mix_parts.append((ma, mb))
            pre_grads.append(pre_grad)
            gated_inners.append(gated_inner)
    returned = home(home_parts)
    if not lean:
        mix_near = jnp.stack([m[0].reshape(-1, rows, width) for m in mix_parts], axis=1)
        mix_far = jnp.stack([m[1].reshape(-1, rows, width) for m in mix_parts], axis=1)
        mix_far, returned = lax.optimization_barrier((mix_far, returned))
        mix_near = add(mix_near, core_flip(mix_far))
        mix_parts = list(reduce_peers(mix_near))
        by_chunk = jnp.stack([g.reshape(2, -1, rows, half) for g in gated_inners], axis=2)
        by_chunk = by_chunk.reshape(2, -1, half)
        down_grad = dot_rows(by_chunk[0], dy_near.reshape(-1, width)) + dot_rows(
            by_chunk[1], dy_far.reshape(-1, width)
        )
        n2_all = jnp.concatenate([part[:, :width] for part in n2_sets], axis=0)
        pre_all = jnp.concatenate(pre_grads, axis=0)
        w1_grad = dot_rows(n2_all, pre_all)
    w1_grad = w1_grad.astype(BF)
    w1_grad, returned = lax.optimization_barrier((w1_grad, returned))
    token_grads = returned[:, :width]
    gg = returned[:, width : width + expert_total * n_dp].reshape(rows, expert_total, n_dp)
    gg = jnp.sum(gg, axis=-1)
    mixed = home(mix_parts)
    down_grad = down_grad.reshape(local_count, ff_part, width)
    w1_grad = walk_swap(w1_grad.reshape(n_dp, cols, -1), tables)
    w1_grad = (
        w1_grad.reshape(n_dp, cols, 2, local_count, ff_part)
        .transpose(2, 3, 1, 0, 4)
        .reshape(2, local_count, cols, ff)
        .astype(F32)
    )
    weighted = gates * gg
    logit_bf = (weighted - gates * jnp.sum(weighted, axis=-1, keepdims=True)).astype(BF)
    router_grad = dot_rows(normed_two, logit_bf)
    normed_two_grad = token_grads + dot(logit_bf, wr_all)
    _, norm_two_back = jax.vjp(rms_scale, hidden_one, gain_two)
    hidden_part, norm_two_grad = norm_two_back(normed_two_grad)
    hidden_grad = cotangent.astype(F32) + hidden_part
    attn_grad_bf = hidden_grad.astype(BF)
    output_grad = scatter(dot_rows(attended, attn_grad_bf).astype(BF), BOTH).astype(F32)
    attended_grad = dot_t(attn_grad_bf, wo_all).astype(BF)
    attended_grad = swap(attended_grad.reshape(rows, n_dp, cols).transpose(1, 0, 2), "dp")
    attended_grad = attended_grad.reshape(-1, cols)

    query_grad, key_grad, value_grad = attend_back(
        query_bf, key_bf, value_bf, bias, attended_grad, score_scale
    )
    hidden_late, query_grad = lax.optimization_barrier((hidden_one, query_grad))
    block_out = (hidden_late + mixed).astype(BF)
    query_grad = query_grad.reshape(-1, cols // HD, HD)
    key_grad = key_grad.reshape(-1, cols // HD, HD)
    query_flat_grad, query_gain_grad = query_back(query_grad)
    key_flat_grad, key_gain_grad = key_back(key_grad)
    qkv_grad = jnp.concatenate(
        [query_flat_grad.astype(BF), key_flat_grad.astype(BF), value_grad],
        axis=1,
    )
    walk_grad = pick_rows(qkv_grad.reshape(n_dp, rows, 3 * cols), member_of_walk)
    part_grad = dot_t(walk_grad.reshape(-1, 3 * cols), qkv)
    walk_in = pick_rows(seq_tokens.reshape(n_dp, rows, width), member_of_walk)
    seq_in = walk_in.reshape(-1, width).astype(F32)
    seq_scale = lax.rsqrt(jnp.mean(seq_in * seq_in, axis=-1, keepdims=True) + norm_eps)
    norm_one_grad = jnp.sum(part_grad * (seq_in * seq_scale), axis=0)
    part_bf = part_grad.astype(BF).reshape(n_dp // 2, 2, rows, width)
    sums = []
    for step in range(n_dp // 2):
        sums.append(add(part_bf[step, 0], flip(part_bf[step, 1], "dp", 1)))
    normed_one_grad = home(sums)
    _, norm_one_back = jax.vjp(lambda v: rms_scale(v, gain_one), inputs)
    (input_part,) = norm_one_back(normed_one_grad)
    grad_tokens = (hidden_grad + input_part).astype(BF)
    qkv_w = dot_rows(normed_one, qkv_grad).astype(BF)
    qkv_w = qkv_w.reshape(n_dp, n_ex, wrows, 3 * cols).transpose(1, 0, 2, 3)
    qkv_w = swap(qkv_w, "expert").astype(F32).sum(axis=0).astype(BF)
    qkv_w = swap(qkv_w, "dp").reshape(n_dp, wrows, 3, cols).transpose(2, 1, 0, 3)
    qkv_w = qkv_w.reshape(3, wrows, width).astype(F32)

    small = jnp.concatenate(
        [
            norm_one_grad.reshape(n_all, -1),
            norm_two_grad.reshape(n_all, -1),
            query_gain_grad.reshape(n_all, -1),
            key_gain_grad.reshape(n_all, -1),
            router_grad.reshape(n_all, -1),
        ],
        axis=1,
    )
    small = jnp.sum(swap(small, BOTH).reshape(n_all, -1), axis=0)
    return (
        block_out,
        grad_tokens,
        small[:gw],
        qkv_w[0],
        qkv_w[1],
        qkv_w[2],
        output_grad,
        small[2 * gw : 2 * gw + hw],
        small[2 * gw + hw : 2 * gw + 2 * hw],
        small[gw : 2 * gw],
        small[2 * gw + 2 * hw :].reshape(wrows, expert_total),
        w1_grad[0],
        w1_grad[1],
        down_grad,
    )


def solution(mesh):
    rows2 = P(("dp", "expert"), None)
    rows1 = P(("dp", "expert"))
    experts = P("expert", "dp", None)
    return jax.shard_map(
        on_device,
        mesh=mesh,
        in_specs=(rows2, rows2, P(), P(), rows2, rows1, rows2, rows2, rows2, rows2)
        + (rows1, rows1, rows1, rows2, experts, experts, experts),
        out_specs=(rows2, rows2, rows1, rows2, rows2, rows2, rows2)
        + (rows1, rows1, rows1, rows2, experts, experts, experts),
        check_vma=False,
    )
```

```python
from functools import partial
import math

import jax
import jax.numpy as jnp
from jax import lax
from jax.experimental import pallas as pl
from jax.experimental.pallas import tpu as pltpu
from jax.sharding import PartitionSpec as P


HD = 128

norm_eps = 1e-06
rope_base = 10000.0
BF = jnp.bfloat16
F32 = jnp.float32


def rms_scale(features, gain_vec):
    return (
        features
        * lax.rsqrt(jnp.mean(features * features, axis=-1, keepdims=True) + norm_eps)
        * gain_vec
    )


def rotary(features, angles):
    half_dim = features.shape[-1] // 2
    cosine = jnp.cos(angles)[:, None, :]
    sine_part = jnp.sin(angles)[:, None, :]
    front_half = features[..., :half_dim]
    back_half = features[..., half_dim:]
    return jnp.concatenate(
        [front_half * cosine - back_half * sine_part, back_half * cosine + front_half * sine_part],
        axis=-1,
    )


def head_piece(angles, flat_vals, gain_vec):
    count = flat_vals.shape[0]
    shaped = flat_vals.reshape(count, -1, HD)
    return rotary(rms_scale(shaped, gain_vec), angles)


def dot(left_mat, right_mat):
    return jnp.dot(left_mat, right_mat, preferred_element_type=F32)


def dot_rows(left_mat, right_mat):
    return lax.dot_general(
        left_mat, right_mat, (((0,), (0,)), ((), ())), preferred_element_type=F32
    )


def dot_t(left_mat, right_mat):
    return lax.dot_general(
        left_mat, right_mat, (((1,), (1,)), ((), ())), preferred_element_type=F32
    )


BOTH = ("dp", "expert")


def swap(blocks, axes):
    return lax.all_to_all(blocks, axes, split_axis=0, concat_axis=0, tiled=True)


def gather(shard, axes):
    return lax.all_gather(shard, axes, axis=0, tiled=True)


def scatter(partial_sum, axes):
    return lax.psum_scatter(partial_sum, axes, scatter_dimension=0, tiled=True)


def ring_order(size):
    return list(range(0, size, 2)) + list(range(1, size, 2))[::-1]


def ring_perm(n_dp, steps):
    order = ring_order(n_dp // 2)
    size = len(order)
    pairs = []
    for spot in range(size):
        for inner in range(2):
            target = order[(spot + steps) % size]
            pairs.append((order[spot] * 2 + inner, target * 2 + inner))
    return pairs


def ring_shift(vals, steps):
    return lax.ppermute(vals, "dp", ring_perm(lax.axis_size("dp"), steps))


def flip(vals, axis, bit):
    size = lax.axis_size(axis)
    return lax.ppermute(vals, axis, [(i, i ^ bit) for i in range(size)])


def core_flip(vals):
    return flip(vals, "expert", 1)


def cross(vals, inner, bits):
    if inner == 0:
        return flip(vals, "expert", bits)
    if bits == 0:
        return flip(vals, "dp", 1)
    n_ex = lax.axis_size("expert")
    size = lax.axis_size("dp") * n_ex
    pairs = [(i, ((i // n_ex) ^ 1) * n_ex + ((i % n_ex) ^ bits)) for i in range(size)]
    return lax.ppermute(vals, BOTH, pairs)


def peers():
    size = lax.axis_size("expert")
    return [(inner, bits) for bits in range(0, size, 2) for inner in range(2)][1:]


def ring_blocks(vals):
    blocks = [vals]
    for step in range(1, lax.axis_size("dp") // 2):
        blocks.append(ring_shift(after(vals, blocks[1]) if step == 2 else vals, step))
    return blocks


def after(vals, *others):
    return lax.optimization_barrier((vals,) + others)[0]


def pick_rows(vals, index):
    return vals.at[index].get(mode="promise_in_bounds")


def add32(left, right):
    return left.astype(F32) + right.astype(F32)


def add(left, right):
    return (left.astype(F32) + right.astype(F32)).astype(left.dtype)


def x_flip(vals):
    return flip(vals, "expert", 2)


def y_flip(vals):
    return flip(vals, "dp", 1)


def split_at(width):
    return width // 256 * 128


def gather_peers(vals):
    if lax.axis_size("expert") != 4:
        return jnp.stack([vals] + [cross(vals, *peer) for peer in peers()])
    cut = split_at(vals.shape[-1])
    left, right = vals[..., :cut], vals[..., cut:]
    left_y, right_x = y_flip(left), x_flip(right)
    left_pair, right_pair = jnp.stack([left, left_y]), jnp.stack([right, right_x])
    left_far, right_far = x_flip(left_pair), y_flip(right_pair)
    return jnp.stack(
        [
            vals,
            jnp.concatenate([left_y, right_far[0]], axis=-1),
            jnp.concatenate([left_far[0], right_x], axis=-1),
            jnp.concatenate([left_far[1], right_far[1]], axis=-1),
        ]
    )


def reduce_peers(vals):
    if lax.axis_size("expert") == 4:
        cut = split_at(vals.shape[-1])
        own, at_y, at_x, at_xy = vals[0], vals[1], vals[2], vals[3]
        left = x_flip(jnp.stack([at_x[..., :cut], at_xy[..., :cut]]))
        right = y_flip(jnp.stack([at_y[..., cut:], at_xy[..., cut:]]))
        left_y = add(at_y[..., :cut], left[1])
        right_x = add(at_x[..., cut:], right[1])
        left_y, right_x = y_flip(left_y), x_flip(right_x)
        left = add(add32(own[..., :cut], left[0]), left_y).astype(vals.dtype)
        right = add(add32(own[..., cut:], right[0]), right_x).astype(vals.dtype)
        return jnp.concatenate([left, right], axis=-1)
    total = vals[0].astype(F32)
    for spot, peer in enumerate(peers()):
        total = total + cross(vals[spot + 1], *peer).astype(F32)
    return total.astype(vals.dtype)


def walk_tables(n_dp):
    ring = ring_order(n_dp // 2)
    size = len(ring)
    ring_arr = jnp.array(ring, jnp.int32)
    spot_arr = jnp.array([ring.index(i) for i in range(size)], jnp.int32)
    member = lax.axis_index("dp")
    my_spot = spot_arr[member // 2]
    walk = jnp.arange(n_dp, dtype=jnp.int32)
    inner = (member % 2) ^ (walk % 2)
    source = ring_arr[(my_spot - walk // 2) % size] * 2 + inner
    target = ring_arr[(my_spot + walk // 2) % size] * 2 + inner
    step_of = ((my_spot - spot_arr[walk // 2]) % size) * 2 + inner
    return source, target, step_of


def walk_perm(n_dp, index):
    pairs = ring_perm(n_dp, index // 2)
    return [(src, dst ^ (index % 2)) for src, dst in pairs]


def walk_swap(blocks, tables, wait_for=None):
    n_dp = blocks.shape[0]
    _, target, step_of = tables
    moved = []
    for index in range(n_dp):
        block = lax.dynamic_index_in_dim(blocks, target[index], 0, keepdims=False)
        if index:
            block = lax.ppermute(block, "dp", walk_perm(n_dp, index))
        moved.append(block)
    if wait_for is not None:
        moved = [after(block, wait_for) for block in moved]
    return pick_rows(jnp.stack(moved), step_of)


def home(parts):
    total = parts[0].astype(F32)
    for step in range(1, len(parts)):
        total = total + ring_shift(parts[step], -step).astype(F32)
    return total


def expert_kernel(halves, width, xa, xb, ya, yb, w1, w1t, w2, w2t, pick, place, outs):
    ma, mb, ra, rb, pre_out, inner_out = outs
    step = pl.program_id(0)
    first = step < halves
    x_all = jnp.where(first, xa[...], xb[...])
    dy = jnp.where(first, ya[...], yb[...]).reshape(x_all.shape[0], width)
    x = x_all[:, :width]
    half = w2.shape[0]
    gates = dot(x_all[:, width:], pick[...])
    pre = dot(x, w1[...])
    gate_val, up_val = pre[:, :half], pre[:, half:]
    sig = 1.0 / (1.0 + jnp.exp(-gate_val))
    silu = gate_val * sig
    inner = (silu * up_val).astype(BF).astype(F32)
    gated = (gates * inner).astype(BF)
    inner_out[...] = gated
    mix = dot(gated, w2[...]).astype(BF)
    back = dot(dy, w2t[...])
    prod = inner * back
    prod_hi = prod.astype(BF)
    prod_lo = (prod - prod_hi.astype(F32)).astype(BF)
    gate_grad = (dot(prod_hi, place[...]) + dot(prod_lo, place[...])).astype(BF)
    inner_grad = gates * back
    gate_pre = (inner_grad * up_val * sig * (1.0 + gate_val * (1.0 - sig))).astype(BF)
    up_pre = (inner_grad * silu).astype(BF)
    pre_out[:, :half] = gate_pre
    pre_out[:, half:] = up_pre
    rows = (dot(gate_pre, w1t[:half, :]) + dot(up_pre, w1t[half:, :])).astype(BF)

    @pl.when(first)
    def _():
        ma[...] = mix
        ra[:, :width] = rows
        ra[:, width:] = gate_grad

    @pl.when(jnp.logical_not(first))
    def _():
        mb[...] = mix
        rb[:, :width] = rows
        rb[:, width:] = gate_grad


def experts(chunk, xa, xb, ya, yb, w1, w1t, w2, w2t, pick, place):
    count, wide = xa.shape
    rows, width = ya.shape[2:]
    half = w2.shape[0]
    tile = 2 * rows
    halves = count // tile
    front = lambda i: (jnp.minimum(i, halves - 1), 0)
    rear = lambda i: (jnp.maximum(i - halves, 0), 0)
    whole = lambda arr: pl.BlockSpec(arr.shape, lambda i: (0, 0), pipeline_mode=pl.Buffered(1))
    back_wide = width + place.shape[1]

    def body(xa, xb, ya, yb, w1, w1t, w2, w2t, pick, place, *outs):
        expert_kernel(halves, width, xa, xb, ya, yb, w1, w1t, w2, w2t, pick, place, outs)

    flops = 2 * 2 * count * width * half * 6
    return pl.pallas_call(
        body,
        grid=(2 * halves,),
        in_specs=[
            pl.BlockSpec((tile, wide), front),
            pl.BlockSpec((tile, wide), rear),
            pl.BlockSpec((2, None, rows, width), lambda i: (front(i)[0], chunk, 0, 0)),
            pl.BlockSpec((2, None, rows, width), lambda i: (rear(i)[0], chunk, 0, 0)),
        ]
        + [whole(arr) for arr in (w1, w1t, w2, w2t, pick, place)],
        out_specs=[
            pl.BlockSpec((tile, width), front),
            pl.BlockSpec((tile, width), rear),
            pl.BlockSpec((tile, back_wide), front),
            pl.BlockSpec((tile, back_wide), rear),
            pl.BlockSpec((tile, 2 * half), lambda i: (i, 0)),
            pl.BlockSpec((tile, half), lambda i: (i, 0)),
        ],
        out_shape=[
            jax.ShapeDtypeStruct((count, width), BF),
            jax.ShapeDtypeStruct((count, width), BF),
            jax.ShapeDtypeStruct((count, back_wide), BF),
            jax.ShapeDtypeStruct((count, back_wide), BF),
            jax.ShapeDtypeStruct((2 * count, 2 * half), BF),
            jax.ShapeDtypeStruct((2 * count, half), BF),
        ],
        cost_estimate=pl.CostEstimate(
            flops=flops, transcendentals=2 * count * half, bytes_accessed=20 * count * width
        ),
        name="experts",
    )(xa, xb, ya, yb, w1, w1t, w2, w2t, pick, place)


def attend_kernel(scale, q, k, v, bias, out):
    scores = dot_t(q[...], k[...]) * scale + bias[...]
    weights = jnp.exp(scores - jnp.max(scores, axis=-1, keepdims=True))
    probs = (weights / jnp.sum(weights, axis=-1, keepdims=True)).astype(BF)
    out[...] = dot(probs, v[...]).astype(BF)


def attend(q, k, v, bias, scale):
    count, cols = q.shape
    tile = min(256, count)
    mine = pl.BlockSpec((tile, HD), lambda h, i: (i, h))
    full = pl.BlockSpec((count, HD), lambda h, i: (0, h))
    return pl.pallas_call(
        partial(attend_kernel, scale),
        grid=(cols // HD, count // tile),
        in_specs=[mine, full, full, pl.BlockSpec((1, count), lambda h, i: (0, 0))],
        out_specs=mine,
        out_shape=jax.ShapeDtypeStruct((count, cols), BF),
        cost_estimate=pl.CostEstimate(
            flops=4 * count * count * cols,
            transcendentals=count * count * cols // HD,
            bytes_accessed=8 * count * cols,
        ),
        name="attend",
    )(q, k, v, bias)


def attend_back_kernel(scale, q, k, v, bias, grad, dq, dk, dv, dk_sum, dv_sum):
    step = pl.program_id(1)
    scores = dot_t(q[...], k[...]) * scale + bias[...]
    weights = jnp.exp(scores - jnp.max(scores, axis=-1, keepdims=True))
    probs = weights / jnp.sum(weights, axis=-1, keepdims=True)
    prob_grad = dot_t(grad[...], v[...])
    mean = jnp.sum(probs * prob_grad, axis=-1, keepdims=True)
    score_grad = (probs * (prob_grad - mean)).astype(BF)
    dq[...] = dot(score_grad, k[...]) * scale
    dk_part = dot_rows(score_grad, q[...]) * scale
    dv_part = dot_rows(probs.astype(BF), grad[...])

    @pl.when(step == 0)
    def _():
        dk_sum[...] = dk_part
        dv_sum[...] = dv_part

    @pl.when(step > 0)
    def _():
        dk_sum[...] += dk_part
        dv_sum[...] += dv_part

    @pl.when(step == pl.num_programs(1) - 1)
    def _():
        dk[...] = dk_sum[...]
        dv[...] = dv_sum[...].astype(BF)


def attend_back(q, k, v, bias, grad, scale):
    count, cols = q.shape
    tile = min(256, count)
    mine = pl.BlockSpec((tile, HD), lambda h, i: (i, h))
    full = pl.BlockSpec((count, HD), lambda h, i: (0, h))
    return pl.pallas_call(
        partial(attend_back_kernel, scale),
        grid=(cols // HD, count // tile),
        in_specs=[mine, full, full, pl.BlockSpec((1, count), lambda h, i: (0, 0)), mine],
        out_specs=[mine, full, full],
        out_shape=[
            jax.ShapeDtypeStruct((count, cols), F32),
            jax.ShapeDtypeStruct((count, cols), F32),
            jax.ShapeDtypeStruct((count, cols), BF),
        ],
        scratch_shapes=[pltpu.VMEM((count, HD), F32), pltpu.VMEM((count, HD), F32)],
        cost_estimate=pl.CostEstimate(
            flops=10 * count * count * cols,
            transcendentals=count * count * cols // HD,
            bytes_accessed=20 * count * cols,
        ),
        name="attend_back",
    )(q, k, v, bias, grad)


def lanes(count):
    return -(-count // 128) * 128


def on_device(
    tokens,
    cotangent,
    lengths,
    piece_order,
    routes,
    attn_gain,
    w_query,
    w_key,
    w_value,
    w_output,
    query_gain,
    key_gain,
    moe_gain,
    w_router,
    w_gate,
    w_up,
    w_down,
):
    rows, width = tokens.shape
    seq_id = lax.axis_index("expert")
    n_dp = lax.axis_size("dp")
    n_ex = lax.axis_size("expert")
    n_all = n_dp * n_ex
    local_count, _, ff = w_gate.shape
    expert_total = local_count * n_ex
    ff_part = ff // n_dp
    cols = width // n_dp
    wrows = w_query.shape[0]
    score_scale = 1.0 / math.sqrt(HD)

    seq_tokens = gather(tokens, "dp")
    member = lax.axis_index("dp")
    tables = walk_tables(n_dp)
    member_of_walk = tables[0]
    qkv = jnp.stack([w_query, w_key, w_value]).astype(BF).reshape(3, wrows, n_dp, cols)
    qkv = swap(qkv.transpose(2, 1, 0, 3), "dp")
    gains = jnp.concatenate(
        [attn_gain, moe_gain, query_gain, key_gain, w_router.T.reshape(-1)]
    )
    gains = after(gains, qkv)
    gains_all = swap(jnp.broadcast_to(gains, (n_all, gains.shape[0])), BOTH)
    gw, hw = attn_gain.shape[0], query_gain.shape[0]
    gain_one = gains_all[:, :gw].reshape(-1)
    gain_two = gains_all[:, gw : 2 * gw].reshape(-1)
    gain_q = gains_all[:, 2 * gw : 2 * gw + hw].reshape(-1)
    gain_k = gains_all[:, 2 * gw + hw : 2 * gw + 2 * hw].reshape(-1)
    wr_all = gains_all[:, 2 * gw + 2 * hw :].reshape(n_all, expert_total, wrows)
    wr_all = wr_all.transpose(1, 0, 2).reshape(expert_total, width).astype(BF)

    qkv = qkv.reshape(1, n_dp, wrows, 3 * cols)
    bit = 1
    while bit < n_ex:
        qkv = jnp.concatenate([qkv, flip(qkv, "expert", bit)], axis=0)
        bit *= 2
    qkv = pick_rows(qkv, seq_id ^ jnp.arange(n_ex, dtype=jnp.int32))
    qkv = qkv.transpose(1, 0, 2, 3).reshape(width, 3 * cols)
    wo_all = gather(w_output.astype(BF), BOTH)
    w1 = jnp.stack([w_gate, w_up]).astype(BF).reshape(2, local_count, cols, n_dp, ff_part)
    w1 = w1.transpose(3, 2, 0, 1, 4).reshape(n_dp, cols, -1)
    w1 = after(w1, gains_all)
    dy_ring = jnp.stack(ring_blocks(after(cotangent, gains_all)))
    w1 = walk_swap(w1, tables)
    w1 = w1.reshape(width, -1)
    w2 = w_down.astype(BF).reshape(local_count * ff_part, width)
    half = local_count * ff_part
    w1t, w2t = w1.T, w2.T
    dy_near = gather_peers(dy_ring)
    dy_far = core_flip(dy_near)

    seq_in = seq_tokens.astype(F32)
    normed_one = rms_scale(seq_in, gain_one).astype(BF)
    qkv_flat = dot(normed_one, qkv)
    offsets = jnp.arange(rows, dtype=jnp.int32)
    position = (piece_order[seq_id][:, None] * rows + offsets[None, :]).reshape(-1)
    visible = position < lengths[seq_id]
    half_dim = HD // 2
    frequency = rope_base ** (-(jnp.arange(half_dim, dtype=F32) * 2.0 / HD))
    angles = position.astype(F32)[:, None] * frequency[None, :]
    query_rot, query_back = jax.vjp(partial(head_piece, angles), qkv_flat[:, :cols], gain_q)
    key_rot, key_back = jax.vjp(partial(head_piece, angles), qkv_flat[:, cols : 2 * cols], gain_k)
    query_bf = query_rot.astype(BF).reshape(-1, cols)
    key_bf = key_rot.astype(BF).reshape(-1, cols)
    value_bf = qkv_flat[:, 2 * cols :].astype(BF)
    bias = jnp.where(visible, 0.0, -jnp.inf).astype(F32)[None, :]
    attended = attend(query_bf, key_bf, value_bf, bias, score_scale)
    attended = swap(attended.reshape(n_dp, rows, cols), "dp")
    attended = attended.transpose(1, 0, 2).reshape(rows, width)
    attended, w1, w1t, w2t = lax.optimization_barrier((attended, w1, w1t, w2t))

    inputs = tokens.astype(F32)
    hidden_one = inputs + dot(attended, wo_all)
    normed_two = rms_scale(hidden_one, gain_two).astype(BF)
    router_logits = dot_t(normed_two, wr_all)
    expert_ids = jnp.arange(expert_total, dtype=jnp.int32)
    routed = jnp.any(routes[:, :, None] == expert_ids[None, None, :], axis=1)
    masked_logits = jnp.where(routed, router_logits, -jnp.inf)
    gates = jax.nn.softmax(masked_logits, axis=-1)
    gates_hi = gates.astype(BF)
    gates_lo = (gates - gates_hi.astype(F32)).astype(BF)
    spare = lanes(2 * expert_total) - 2 * expert_total
    payload = jnp.concatenate(
        [normed_two, gates_hi, gates_lo, jnp.zeros((rows, spare), BF)], axis=1
    )
    unit = jnp.arange(half, dtype=jnp.int32) // ff_part + seq_id * local_count
    gate_col = jnp.arange(lanes(2 * expert_total), dtype=jnp.int32)
    pick = (
        (gate_col[:, None] == unit[None, :]) | (gate_col[:, None] == unit[None, :] + expert_total)
    ).astype(BF)
    grad_col = jnp.arange(lanes(expert_total * n_dp), dtype=jnp.int32)
    place = (grad_col[None, :] == (unit * n_dp + member)[:, None]).astype(BF)

    lean = n_all * rows > 4096
    n2_sets, mix_parts, home_parts, pre_grads, gated_inners = [], [], [], [], []
    w1_grad, down_grad = 0.0, 0.0
    for step, block in enumerate(ring_blocks(payload)):
        near = gather_peers(block).reshape(-1, block.shape[-1])
        far = core_flip(near)
        ma, mb, ra, rb, pre_grad, gated_inner = experts(
            step, near, far, dy_near, dy_far, w1, w1t, w2, w2t, pick, place
        )
        part = add(ra, core_flip(rb)).reshape(-1, rows, ra.shape[1])
        home_parts.append(reduce_peers(part))
        if lean:
            mix_parts.append(reduce_peers(add(ma, core_flip(mb)).reshape(-1, rows, width)))
            cut = pre_grad.shape[0] // 2
            w1_grad = w1_grad + dot_rows(near[:, :width], pre_grad[:cut])
            w1_grad = w1_grad + dot_rows(far[:, :width], pre_grad[cut:])
            down_grad = down_grad + dot_rows(gated_inner[:cut], dy_near[:, step].reshape(-1, width))
            down_grad = down_grad + dot_rows(gated_inner[cut:], dy_far[:, step].reshape(-1, width))
            w1_grad, down_grad, dy_near, dy_far, mix_parts, home_parts, payload = (
                lax.optimization_barrier(
                    (w1_grad, down_grad, dy_near, dy_far, mix_parts, home_parts, payload)
                )
            )
        else:
            n2_sets += [near, far]
            mix_parts.append((ma, mb))
            pre_grads.append(pre_grad)
            gated_inners.append(gated_inner)
    returned = home(home_parts)
    if not lean:
        mix_near = jnp.stack([m[0].reshape(-1, rows, width) for m in mix_parts], axis=1)
        mix_far = jnp.stack([m[1].reshape(-1, rows, width) for m in mix_parts], axis=1)
        mix_far = after(mix_far, returned)
        mix_near = add(mix_near, core_flip(mix_far))
        mix_parts = list(reduce_peers(mix_near))
        by_chunk = jnp.stack([g.reshape(2, -1, rows, half) for g in gated_inners], axis=2)
        by_chunk = by_chunk.reshape(2, -1, half)
        down_grad = dot_rows(by_chunk[0], dy_near.reshape(-1, width)) + dot_rows(
            by_chunk[1], dy_far.reshape(-1, width)
        )
        n2_all = jnp.concatenate([part[:, :width] for part in n2_sets], axis=0)
        pre_all = jnp.concatenate(pre_grads, axis=0)
        w1_grad = dot_rows(n2_all, pre_all)
    w1_grad = w1_grad.astype(BF)
    w1_grad = after(w1_grad, returned)
    token_grads = returned[:, :width]
    gg = returned[:, width : width + expert_total * n_dp].reshape(rows, expert_total, n_dp)
    gg = jnp.sum(gg, axis=-1)
    mixed = home(mix_parts)
    down_grad = down_grad.reshape(local_count, ff_part, width)
    weighted = gates * gg
    logit_bf = (weighted - gates * jnp.sum(weighted, axis=-1, keepdims=True)).astype(BF)
    router_grad = dot_rows(normed_two, logit_bf)
    normed_two_grad = token_grads + dot(logit_bf, wr_all)
    _, norm_two_back = jax.vjp(rms_scale, hidden_one, gain_two)
    hidden_part, norm_two_grad = norm_two_back(normed_two_grad)
    hidden_grad = cotangent.astype(F32) + hidden_part
    attn_grad_bf = hidden_grad.astype(BF)
    output_grad = scatter(dot_rows(attended, attn_grad_bf).astype(BF), BOTH).astype(F32)
    attended_grad = dot_t(attn_grad_bf, wo_all).astype(BF)
    attended_grad = swap(attended_grad.reshape(rows, n_dp, cols).transpose(1, 0, 2), "dp")
    attended_grad = attended_grad.reshape(-1, cols)

    query_grad, key_grad, value_grad = attend_back(
        query_bf, key_bf, value_bf, bias, attended_grad, score_scale
    )
    block_out = (after(hidden_one, query_grad) + mixed).astype(BF)
    query_grad = query_grad.reshape(-1, cols // HD, HD)
    key_grad = key_grad.reshape(-1, cols // HD, HD)
    query_flat_grad, query_gain_grad = query_back(query_grad)
    key_flat_grad, key_gain_grad = key_back(key_grad)
    qkv_grad = jnp.concatenate(
        [query_flat_grad.astype(BF), key_flat_grad.astype(BF), value_grad],
        axis=1,
    )
    walk_grad = pick_rows(qkv_grad.reshape(n_dp, rows, 3 * cols), member_of_walk)
    part_grad = dot_t(walk_grad.reshape(-1, 3 * cols), qkv)
    walk_in = pick_rows(seq_tokens.reshape(n_dp, rows, width), member_of_walk)
    seq_in = walk_in.reshape(-1, width).astype(F32)
    seq_scale = lax.rsqrt(jnp.mean(seq_in * seq_in, axis=-1, keepdims=True) + norm_eps)
    norm_one_grad = jnp.sum(part_grad * (seq_in * seq_scale), axis=0)
    part_bf = part_grad.astype(BF).reshape(n_dp // 2, 2, rows, width)
    sums = []
    for step in range(n_dp // 2):
        sums.append(add(part_bf[step, 0], flip(part_bf[step, 1], "dp", 1)))
    normed_one_grad = home(sums)
    w1_grad = walk_swap(w1_grad.reshape(n_dp, cols, -1), tables, sums[-1])

    def unpack(blocks):
        blocks = blocks.reshape(n_dp, cols, local_count, ff_part).transpose(2, 1, 0, 3)
        return blocks.reshape(local_count, cols, ff).astype(F32)

    gate_w_grad, up_w_grad = unpack(w1_grad[:, :, :half]), unpack(w1_grad[:, :, half:])
    _, norm_one_back = jax.vjp(lambda v: rms_scale(v, gain_one), inputs)
    (input_part,) = norm_one_back(normed_one_grad)
    grad_tokens = (hidden_grad + input_part).astype(BF)
    qkv_w = dot_rows(normed_one, qkv_grad).astype(BF)
    qkv_w = qkv_w.reshape(n_dp, n_ex, wrows, 3 * cols).transpose(1, 0, 2, 3)
    qkv_w = swap(qkv_w, "expert").astype(F32).sum(axis=0).astype(BF)
    qkv_w = swap(qkv_w, "dp").reshape(n_dp, wrows, 3, cols).transpose(2, 1, 0, 3)
    qkv_w = qkv_w.reshape(3, wrows, width).astype(F32)

    small = jnp.concatenate(
        [
            norm_one_grad.reshape(n_all, -1),
            norm_two_grad.reshape(n_all, -1),
            query_gain_grad.reshape(n_all, -1),
            key_gain_grad.reshape(n_all, -1),
            router_grad.reshape(n_all, -1),
        ],
        axis=1,
    )
    small = jnp.sum(swap(small, BOTH).reshape(n_all, -1), axis=0)
    return (
        block_out,
        grad_tokens,
        small[:gw],
        qkv_w[0],
        qkv_w[1],
        qkv_w[2],
        output_grad,
        small[2 * gw : 2 * gw + hw],
        small[2 * gw + hw : 2 * gw + 2 * hw],
        small[gw : 2 * gw],
        small[2 * gw + 2 * hw :].reshape(wrows, expert_total),
        gate_w_grad,
        up_w_grad,
        down_grad,
    )


def solution(mesh):
    rows2 = P(("dp", "expert"), None)
    rows1 = P(("dp", "expert"))
    experts = P("expert", "dp", None)
    return jax.shard_map(
        on_device,
        mesh=mesh,
        in_specs=(rows2, rows2, P(), P(), rows2, rows1, rows2, rows2, rows2, rows2)
        + (rows1, rows1, rows1, rows2, experts, experts, experts),
        out_specs=(rows2, rows2, rows1, rows2, rows2, rows2, rows2)
        + (rows1, rows1, rows1, rows2, experts, experts, experts),
        check_vma=False,
    )
```

```python
from functools import partial
import math

import jax
import jax.numpy as jnp
from jax import lax
from jax.experimental import pallas as pl
from jax.experimental.pallas import tpu as pltpu
from jax.sharding import PartitionSpec as P


HD = 128

norm_eps = 1e-06
rope_base = 10000.0
BF = jnp.bfloat16
F32 = jnp.float32


def rms_scale(features, gain_vec):
    return (
        features
        * lax.rsqrt(jnp.mean(features * features, axis=-1, keepdims=True) + norm_eps)
        * gain_vec
    )


def rotary(features, angles):
    half_dim = features.shape[-1] // 2
    cosine = jnp.cos(angles)[:, None, :]
    sine_part = jnp.sin(angles)[:, None, :]
    front_half = features[..., :half_dim]
    back_half = features[..., half_dim:]
    return jnp.concatenate(
        [front_half * cosine - back_half * sine_part, back_half * cosine + front_half * sine_part],
        axis=-1,
    )


def head_piece(angles, flat_vals, gain_vec):
    count = flat_vals.shape[0]
    shaped = flat_vals.reshape(count, -1, HD)
    return rotary(rms_scale(shaped, gain_vec), angles)


def dot(left_mat, right_mat):
    return jnp.dot(left_mat, right_mat, preferred_element_type=F32)


def dot_rows(left_mat, right_mat):
    return lax.dot_general(
        left_mat, right_mat, (((0,), (0,)), ((), ())), preferred_element_type=F32
    )


def dot_t(left_mat, right_mat):
    return lax.dot_general(
        left_mat, right_mat, (((1,), (1,)), ((), ())), preferred_element_type=F32
    )


BOTH = ("dp", "expert")


def swap(blocks, axes):
    return lax.all_to_all(blocks, axes, split_axis=0, concat_axis=0, tiled=True)


def gather(shard, axes):
    return lax.all_gather(shard, axes, axis=0, tiled=True)


def scatter(partial_sum, axes):
    return lax.psum_scatter(partial_sum, axes, scatter_dimension=0, tiled=True)


def ring_order(size):
    return list(range(0, size, 2)) + list(range(1, size, 2))[::-1]


def ring_perm(n_dp, steps):
    order = ring_order(n_dp // 2)
    size = len(order)
    pairs = []
    for spot in range(size):
        for inner in range(2):
            target = order[(spot + steps) % size]
            pairs.append((order[spot] * 2 + inner, target * 2 + inner))
    return pairs


def ring_shift(vals, steps):
    return lax.ppermute(vals, "dp", ring_perm(lax.axis_size("dp"), steps))


def flip(vals, axis, bit):
    size = lax.axis_size(axis)
    return lax.ppermute(vals, axis, [(i, i ^ bit) for i in range(size)])


def core_flip(vals):
    return flip(vals, "expert", 1)


def cross(vals, inner, bits):
    if inner == 0:
        return flip(vals, "expert", bits)
    if bits == 0:
        return flip(vals, "dp", 1)
    n_ex = lax.axis_size("expert")
    size = lax.axis_size("dp") * n_ex
    pairs = [(i, ((i // n_ex) ^ 1) * n_ex + ((i % n_ex) ^ bits)) for i in range(size)]
    return lax.ppermute(vals, BOTH, pairs)


def peers():
    size = lax.axis_size("expert")
    return [(inner, bits) for bits in range(0, size, 2) for inner in range(2)][1:]


def ring_blocks(vals, urgent=False):
    blocks = [vals]
    for step in range(1, lax.axis_size("dp") // 2):
        blocks.append(ring_shift(after(vals, blocks[1]) if urgent and step > 1 else vals, step))
    return blocks


def after(vals, *others):
    return lax.optimization_barrier((vals,) + others)[0]


def pick_rows(vals, index):
    return vals.at[index].get(mode="promise_in_bounds")


def add32(left, right):
    return left.astype(F32) + right.astype(F32)


def add(left, right):
    return (left.astype(F32) + right.astype(F32)).astype(left.dtype)


def x_flip(vals):
    return flip(vals, "expert", 2)


def y_flip(vals):
    return flip(vals, "dp", 1)


def split_at(width):
    return width // 256 * 128


def gather_peers(vals):
    if lax.axis_size("expert") != 4:
        return jnp.stack([vals] + [cross(vals, *peer) for peer in peers()])
    cut = split_at(vals.shape[-1])
    left, right = vals[..., :cut], vals[..., cut:]
    left_y, right_x = y_flip(left), x_flip(right)
    left_pair, right_pair = jnp.stack([left, left_y]), jnp.stack([right, right_x])
    left_far, right_far = x_flip(left_pair), y_flip(right_pair)
    return jnp.stack(
        [
            vals,
            jnp.concatenate([left_y, right_far[0]], axis=-1),
            jnp.concatenate([left_far[0], right_x], axis=-1),
            jnp.concatenate([left_far[1], right_far[1]], axis=-1),
        ]
    )


def reduce_peers(vals):
    if lax.axis_size("expert") == 4:
        cut = split_at(vals.shape[-1])
        own, at_y, at_x, at_xy = vals[0], vals[1], vals[2], vals[3]
        left = x_flip(jnp.stack([at_x[..., :cut], at_xy[..., :cut]]))
        right = y_flip(jnp.stack([at_y[..., cut:], at_xy[..., cut:]]))
        left_y = add(at_y[..., :cut], left[1])
        right_x = add(at_x[..., cut:], right[1])
        left_y, right_x = y_flip(left_y), x_flip(right_x)
        left = add(add32(own[..., :cut], left[0]), left_y).astype(vals.dtype)
        right = add(add32(own[..., cut:], right[0]), right_x).astype(vals.dtype)
        return jnp.concatenate([left, right], axis=-1)
    total = vals[0].astype(F32)
    for spot, peer in enumerate(peers()):
        total = total + cross(vals[spot + 1], *peer).astype(F32)
    return total.astype(vals.dtype)


def walk_tables(n_dp):
    ring = ring_order(n_dp // 2)
    size = len(ring)
    ring_arr = jnp.array(ring, jnp.int32)
    spot_arr = jnp.array([ring.index(i) for i in range(size)], jnp.int32)
    member = lax.axis_index("dp")
    my_spot = spot_arr[member // 2]
    walk = jnp.arange(n_dp, dtype=jnp.int32)
    inner = (member % 2) ^ (walk % 2)
    source = ring_arr[(my_spot - walk // 2) % size] * 2 + inner
    target = ring_arr[(my_spot + walk // 2) % size] * 2 + inner
    step_of = ((my_spot - spot_arr[walk // 2]) % size) * 2 + inner
    return source, target, step_of


def walk_perm(n_dp, index):
    pairs = ring_perm(n_dp, index // 2)
    return [(src, dst ^ (index % 2)) for src, dst in pairs]


def walk_swap(blocks, tables, wait_for=None):
    n_dp = blocks.shape[0]
    _, target, step_of = tables
    moved = []
    for index in range(n_dp):
        block = lax.dynamic_index_in_dim(blocks, target[index], 0, keepdims=False)
        if index:
            block = lax.ppermute(block, "dp", walk_perm(n_dp, index))
        moved.append(block)
    if wait_for is not None:
        moved = [after(block, *wait_for) for block in moved]
    return pick_rows(jnp.stack(moved), step_of)


def home(parts):
    total = parts[0].astype(F32)
    for step in range(1, len(parts)):
        total = total + ring_shift(parts[step], -step).astype(F32)
    return total


def expert_kernel(halves, width, xa, xb, ya, yb, w1, w1t, w2, w2t, pick, place, outs):
    ma, mb, ra, rb, pre_out, inner_out = outs
    step = pl.program_id(0)
    first = step < halves
    x_all = jnp.where(first, xa[...], xb[...])
    dy = jnp.where(first, ya[...], yb[...]).reshape(x_all.shape[0], width)
    x = x_all[:, :width]
    half = w2.shape[0]
    gates = dot(x_all[:, width:], pick[...])
    pre = dot(x, w1[...])
    gate_val, up_val = pre[:, :half], pre[:, half:]
    sig = 1.0 / (1.0 + jnp.exp(-gate_val))
    silu = gate_val * sig
    inner = (silu * up_val).astype(BF).astype(F32)
    gated = (gates * inner).astype(BF)
    inner_out[...] = gated
    mix = dot(gated, w2[...]).astype(BF)
    back = dot(dy, w2t[...])
    prod = inner * back
    prod_hi = prod.astype(BF)
    prod_lo = (prod - prod_hi.astype(F32)).astype(BF)
    gate_grad = (dot(prod_hi, place[...]) + dot(prod_lo, place[...])).astype(BF)
    inner_grad = gates * back
    gate_pre = (inner_grad * up_val * sig * (1.0 + gate_val * (1.0 - sig))).astype(BF)
    up_pre = (inner_grad * silu).astype(BF)
    pre_out[:, :half] = gate_pre
    pre_out[:, half:] = up_pre
    rows = (dot(gate_pre, w1t[:half, :]) + dot(up_pre, w1t[half:, :])).astype(BF)

    @pl.when(first)
    def _():
        ma[...] = mix
        ra[:, :width] = rows
        ra[:, width:] = gate_grad

    @pl.when(jnp.logical_not(first))
    def _():
        mb[...] = mix
        rb[:, :width] = rows
        rb[:, width:] = gate_grad


def experts(chunk, xa, xb, ya, yb, w1, w1t, w2, w2t, pick, place):
    count, wide = xa.shape
    rows, width = ya.shape[2:]
    half = w2.shape[0]
    tile = 2 * rows
    halves = count // tile
    front = lambda i: (jnp.minimum(i, halves - 1), 0)
    rear = lambda i: (jnp.maximum(i - halves, 0), 0)
    whole = lambda arr: pl.BlockSpec(arr.shape, lambda i: (0, 0), pipeline_mode=pl.Buffered(1))
    back_wide = width + place.shape[1]

    def body(xa, xb, ya, yb, w1, w1t, w2, w2t, pick, place, *outs):
        expert_kernel(halves, width, xa, xb, ya, yb, w1, w1t, w2, w2t, pick, place, outs)

    flops = 2 * 2 * count * width * half * 6
    return pl.pallas_call(
        body,
        grid=(2 * halves,),
        in_specs=[
            pl.BlockSpec((tile, wide), front),
            pl.BlockSpec((tile, wide), rear),
            pl.BlockSpec((2, None, rows, width), lambda i: (front(i)[0], chunk, 0, 0)),
            pl.BlockSpec((2, None, rows, width), lambda i: (rear(i)[0], chunk, 0, 0)),
        ]
        + [whole(arr) for arr in (w1, w1t, w2, w2t, pick, place)],
        out_specs=[
            pl.BlockSpec((tile, width), front),
            pl.BlockSpec((tile, width), rear),
            pl.BlockSpec((tile, back_wide), front),
            pl.BlockSpec((tile, back_wide), rear),
            pl.BlockSpec((tile, 2 * half), lambda i: (i, 0)),
            pl.BlockSpec((tile, half), lambda i: (i, 0)),
        ],
        out_shape=[
            jax.ShapeDtypeStruct((count, width), BF),
            jax.ShapeDtypeStruct((count, width), BF),
            jax.ShapeDtypeStruct((count, back_wide), BF),
            jax.ShapeDtypeStruct((count, back_wide), BF),
            jax.ShapeDtypeStruct((2 * count, 2 * half), BF),
            jax.ShapeDtypeStruct((2 * count, half), BF),
        ],
        cost_estimate=pl.CostEstimate(
            flops=flops, transcendentals=2 * count * half, bytes_accessed=20 * count * width
        ),
        name="experts",
    )(xa, xb, ya, yb, w1, w1t, w2, w2t, pick, place)


def attend_kernel(scale, q, k, v, bias, out):
    scores = dot_t(q[...], k[...]) * scale + bias[...]
    weights = jnp.exp(scores - jnp.max(scores, axis=-1, keepdims=True))
    probs = (weights / jnp.sum(weights, axis=-1, keepdims=True)).astype(BF)
    out[...] = dot(probs, v[...]).astype(BF)


def attend(q, k, v, bias, scale):
    count, cols = q.shape
    tile = min(256, count)
    mine = pl.BlockSpec((tile, HD), lambda h, i: (i, h))
    full = pl.BlockSpec((count, HD), lambda h, i: (0, h))
    return pl.pallas_call(
        partial(attend_kernel, scale),
        grid=(cols // HD, count // tile),
        in_specs=[mine, full, full, pl.BlockSpec((1, count), lambda h, i: (0, 0))],
        out_specs=mine,
        out_shape=jax.ShapeDtypeStruct((count, cols), BF),
        cost_estimate=pl.CostEstimate(
            flops=4 * count * count * cols,
            transcendentals=count * count * cols // HD,
            bytes_accessed=8 * count * cols,
        ),
        name="attend",
    )(q, k, v, bias)


def attend_back_kernel(scale, q, k, v, bias, grad, dq, dk, dv, dk_sum, dv_sum):
    step = pl.program_id(1)
    scores = dot_t(q[...], k[...]) * scale + bias[...]
    weights = jnp.exp(scores - jnp.max(scores, axis=-1, keepdims=True))
    probs = weights / jnp.sum(weights, axis=-1, keepdims=True)
    prob_grad = dot_t(grad[...], v[...])
    mean = jnp.sum(probs * prob_grad, axis=-1, keepdims=True)
    score_grad = (probs * (prob_grad - mean)).astype(BF)
    dq[...] = dot(score_grad, k[...]) * scale
    dk_part = dot_rows(score_grad, q[...]) * scale
    dv_part = dot_rows(probs.astype(BF), grad[...])

    @pl.when(step == 0)
    def _():
        dk_sum[...] = dk_part
        dv_sum[...] = dv_part

    @pl.when(step > 0)
    def _():
        dk_sum[...] += dk_part
        dv_sum[...] += dv_part

    @pl.when(step == pl.num_programs(1) - 1)
    def _():
        dk[...] = dk_sum[...]
        dv[...] = dv_sum[...].astype(BF)


def attend_back(q, k, v, bias, grad, scale):
    count, cols = q.shape
    tile = min(256, count)
    mine = pl.BlockSpec((tile, HD), lambda h, i: (i, h))
    full = pl.BlockSpec((count, HD), lambda h, i: (0, h))
    return pl.pallas_call(
        partial(attend_back_kernel, scale),
        grid=(cols // HD, count // tile),
        in_specs=[mine, full, full, pl.BlockSpec((1, count), lambda h, i: (0, 0)), mine],
        out_specs=[mine, full, full],
        out_shape=[
            jax.ShapeDtypeStruct((count, cols), F32),
            jax.ShapeDtypeStruct((count, cols), F32),
            jax.ShapeDtypeStruct((count, cols), BF),
        ],
        scratch_shapes=[pltpu.VMEM((count, HD), F32), pltpu.VMEM((count, HD), F32)],
        cost_estimate=pl.CostEstimate(
            flops=10 * count * count * cols,
            transcendentals=count * count * cols // HD,
            bytes_accessed=20 * count * cols,
        ),
        name="attend_back",
    )(q, k, v, bias, grad)


def lanes(count):
    return -(-count // 128) * 128


def on_device(
    tokens,
    cotangent,
    lengths,
    piece_order,
    routes,
    attn_gain,
    w_query,
    w_key,
    w_value,
    w_output,
    query_gain,
    key_gain,
    moe_gain,
    w_router,
    w_gate,
    w_up,
    w_down,
):
    rows, width = tokens.shape
    seq_id = lax.axis_index("expert")
    n_dp = lax.axis_size("dp")
    n_ex = lax.axis_size("expert")
    n_all = n_dp * n_ex
    local_count, _, ff = w_gate.shape
    expert_total = local_count * n_ex
    ff_part = ff // n_dp
    cols = width // n_dp
    wrows = w_query.shape[0]
    score_scale = 1.0 / math.sqrt(HD)

    seq_tokens = gather(tokens, "dp")
    member = lax.axis_index("dp")
    tables = walk_tables(n_dp)
    member_of_walk = tables[0]
    qkv = jnp.stack([w_query, w_key, w_value]).astype(BF).reshape(3, wrows, n_dp, cols)
    qkv = swap(qkv.transpose(2, 1, 0, 3), "dp")
    gains = jnp.concatenate(
        [attn_gain, moe_gain, query_gain, key_gain, w_router.T.reshape(-1)]
    )
    gains = after(gains, qkv)
    gains_all = swap(jnp.broadcast_to(gains, (n_all, gains.shape[0])), BOTH)
    gw, hw = attn_gain.shape[0], query_gain.shape[0]
    gain_one = gains_all[:, :gw].reshape(-1)
    gain_two = gains_all[:, gw : 2 * gw].reshape(-1)
    gain_q = gains_all[:, 2 * gw : 2 * gw + hw].reshape(-1)
    gain_k = gains_all[:, 2 * gw + hw : 2 * gw + 2 * hw].reshape(-1)
    wr_all = gains_all[:, 2 * gw + 2 * hw :].reshape(n_all, expert_total, wrows)
    wr_all = wr_all.transpose(1, 0, 2).reshape(expert_total, width).astype(BF)

    qkv = qkv.reshape(1, n_dp, wrows, 3 * cols)
    bit = 1
    while bit < n_ex:
        qkv = jnp.concatenate([qkv, flip(qkv, "expert", bit)], axis=0)
        bit *= 2
    qkv = pick_rows(qkv, seq_id ^ jnp.arange(n_ex, dtype=jnp.int32))
    qkv = qkv.transpose(1, 0, 2, 3).reshape(width, 3 * cols)
    wo_all = gather(w_output.astype(BF), BOTH)
    w1 = jnp.stack([w_gate, w_up]).astype(BF).reshape(2, local_count, cols, n_dp, ff_part)
    w1 = w1.transpose(3, 2, 0, 1, 4).reshape(n_dp, cols, -1)
    w1 = after(w1, gains_all)
    dy_ring = jnp.stack(ring_blocks(after(cotangent, gains_all)))
    w1 = walk_swap(w1, tables)
    w1 = w1.reshape(width, -1)
    w2 = w_down.astype(BF).reshape(local_count * ff_part, width)
    half = local_count * ff_part
    w1t, w2t = w1.T, w2.T
    dy_near = gather_peers(dy_ring)
    dy_far = core_flip(dy_near)

    seq_in = seq_tokens.astype(F32)
    normed_one = rms_scale(seq_in, gain_one).astype(BF)
    qkv_flat = dot(normed_one, qkv)
    offsets = jnp.arange(rows, dtype=jnp.int32)
    position = (piece_order[seq_id][:, None] * rows + offsets[None, :]).reshape(-1)
    visible = position < lengths[seq_id]
    half_dim = HD // 2
    frequency = rope_base ** (-(jnp.arange(half_dim, dtype=F32) * 2.0 / HD))
    angles = position.astype(F32)[:, None] * frequency[None, :]
    query_rot, query_back = jax.vjp(partial(head_piece, angles), qkv_flat[:, :cols], gain_q)
    key_rot, key_back = jax.vjp(partial(head_piece, angles), qkv_flat[:, cols : 2 * cols], gain_k)
    query_bf = query_rot.astype(BF).reshape(-1, cols)
    key_bf = key_rot.astype(BF).reshape(-1, cols)
    value_bf = qkv_flat[:, 2 * cols :].astype(BF)
    bias = jnp.where(visible, 0.0, -jnp.inf).astype(F32)[None, :]
    attended = attend(query_bf, key_bf, value_bf, bias, score_scale)
    attended = swap(attended.reshape(n_dp, rows, cols), "dp")
    attended = attended.transpose(1, 0, 2).reshape(rows, width)
    attended, w1, w1t, w2t = lax.optimization_barrier((attended, w1, w1t, w2t))

    inputs = tokens.astype(F32)
    hidden_one = inputs + dot(attended, wo_all)
    normed_two = rms_scale(hidden_one, gain_two).astype(BF)
    router_logits = dot_t(normed_two, wr_all)
    expert_ids = jnp.arange(expert_total, dtype=jnp.int32)
    routed = jnp.any(routes[:, :, None] == expert_ids[None, None, :], axis=1)
    masked_logits = jnp.where(routed, router_logits, -jnp.inf)
    gates = jax.nn.softmax(masked_logits, axis=-1)
    gates_hi = gates.astype(BF)
    gates_lo = (gates - gates_hi.astype(F32)).astype(BF)
    spare = lanes(2 * expert_total) - 2 * expert_total
    payload = jnp.concatenate(
        [normed_two, gates_hi, gates_lo, jnp.zeros((rows, spare), BF)], axis=1
    )
    unit = jnp.arange(half, dtype=jnp.int32) // ff_part + seq_id * local_count
    gate_col = jnp.arange(lanes(2 * expert_total), dtype=jnp.int32)
    pick = (
        (gate_col[:, None] == unit[None, :]) | (gate_col[:, None] == unit[None, :] + expert_total)
    ).astype(BF)
    grad_col = jnp.arange(lanes(expert_total * n_dp), dtype=jnp.int32)
    place = (grad_col[None, :] == (unit * n_dp + member)[:, None]).astype(BF)

    lean = n_all * rows > 4096
    n2_sets, mix_parts, home_parts, pre_grads, gated_inners = [], [], [], [], []
    w1_grad, down_grad = 0.0, 0.0
    for step, block in enumerate(ring_blocks(payload, True)):
        near = gather_peers(block).reshape(-1, block.shape[-1])
        far = core_flip(near)
        ma, mb, ra, rb, pre_grad, gated_inner = experts(
            step, near, far, dy_near, dy_far, w1, w1t, w2, w2t, pick, place
        )
        part = add(ra, core_flip(rb)).reshape(-1, rows, ra.shape[1])
        home_parts.append(reduce_peers(part))
        if lean:
            mix_parts.append(reduce_peers(add(ma, core_flip(mb)).reshape(-1, rows, width)))
            cut = pre_grad.shape[0] // 2
            w1_grad = w1_grad + dot_rows(near[:, :width], pre_grad[:cut])
            w1_grad = w1_grad + dot_rows(far[:, :width], pre_grad[cut:])
            down_grad = down_grad + dot_rows(gated_inner[:cut], dy_near[:, step].reshape(-1, width))
            down_grad = down_grad + dot_rows(gated_inner[cut:], dy_far[:, step].reshape(-1, width))
            w1_grad, down_grad, dy_near, dy_far, mix_parts, home_parts, payload = (
                lax.optimization_barrier(
                    (w1_grad, down_grad, dy_near, dy_far, mix_parts, home_parts, payload)
                )
            )
        else:
            n2_sets += [near, far]
            mix_parts.append((ma, mb))
            pre_grads.append(pre_grad)
            gated_inners.append(gated_inner)
    returned = home(home_parts)
    if not lean:
        mix_near = jnp.stack([m[0].reshape(-1, rows, width) for m in mix_parts], axis=1)
        mix_far = jnp.stack([m[1].reshape(-1, rows, width) for m in mix_parts], axis=1)
        mix_far = after(mix_far, part)
        mix_near = add(mix_near, core_flip(mix_far))
        mix_parts = list(reduce_peers(mix_near))
        by_chunk = jnp.stack([g.reshape(2, -1, rows, half) for g in gated_inners], axis=2)
        by_chunk = by_chunk.reshape(2, -1, half)
        down_grad = dot_rows(by_chunk[0], dy_near.reshape(-1, width)) + dot_rows(
            by_chunk[1], dy_far.reshape(-1, width)
        )
        n2_all = jnp.concatenate([part[:, :width] for part in n2_sets], axis=0)
        pre_all = jnp.concatenate(pre_grads, axis=0)
        w1_grad = dot_rows(n2_all, pre_all)
    w1_grad = w1_grad.astype(BF)
    w1_grad = after(w1_grad, returned)
    token_grads = returned[:, :width]
    gg = returned[:, width : width + expert_total * n_dp].reshape(rows, expert_total, n_dp)
    gg = jnp.sum(gg, axis=-1)
    mixed = home(mix_parts)
    down_grad = down_grad.reshape(local_count, ff_part, width)
    weighted = gates * gg
    logit_bf = (weighted - gates * jnp.sum(weighted, axis=-1, keepdims=True)).astype(BF)
    router_grad = dot_rows(normed_two, logit_bf)
    normed_two_grad = token_grads + dot(logit_bf, wr_all)
    _, norm_two_back = jax.vjp(rms_scale, hidden_one, gain_two)
    hidden_part, norm_two_grad = norm_two_back(normed_two_grad)
    hidden_grad = cotangent.astype(F32) + hidden_part
    attn_grad_bf = hidden_grad.astype(BF)
    output_grad = scatter(dot_rows(attended, attn_grad_bf).astype(BF), BOTH).astype(F32)
    attended_grad = dot_t(attn_grad_bf, wo_all).astype(BF)
    attended_grad = swap(attended_grad.reshape(rows, n_dp, cols).transpose(1, 0, 2), "dp")
    attended_grad = attended_grad.reshape(-1, cols)

    query_grad, key_grad, value_grad = attend_back(
        query_bf, key_bf, value_bf, bias, attended_grad, score_scale
    )
    block_out = (after(hidden_one, query_grad) + mixed).astype(BF)
    query_grad = query_grad.reshape(-1, cols // HD, HD)
    key_grad = key_grad.reshape(-1, cols // HD, HD)
    query_flat_grad, query_gain_grad = query_back(query_grad)
    key_flat_grad, key_gain_grad = key_back(key_grad)
    qkv_grad = jnp.concatenate(
        [query_flat_grad.astype(BF), key_flat_grad.astype(BF), value_grad],
        axis=1,
    )
    walk_grad = pick_rows(qkv_grad.reshape(n_dp, rows, 3 * cols), member_of_walk)
    part_grad = dot_t(walk_grad.reshape(-1, 3 * cols), qkv)
    walk_in = pick_rows(seq_tokens.reshape(n_dp, rows, width), member_of_walk)
    seq_in = walk_in.reshape(-1, width).astype(F32)
    seq_scale = lax.rsqrt(jnp.mean(seq_in * seq_in, axis=-1, keepdims=True) + norm_eps)
    norm_one_grad = jnp.sum(part_grad * (seq_in * seq_scale), axis=0)
    part_bf = part_grad.astype(BF).reshape(n_dp // 2, 2, rows, width)
    sums = []
    for step in range(n_dp // 2):
        sums.append(add(part_bf[step, 0], flip(part_bf[step, 1], "dp", 1)))
    normed_one_grad = home(sums)
    w1_grad = walk_swap(w1_grad.reshape(n_dp, cols, -1), tables, (sums[-1], mix_parts[-1]))

    def unpack(blocks):
        blocks = blocks.reshape(n_dp, cols, local_count, ff_part).transpose(2, 1, 0, 3)
        return blocks.reshape(local_count, cols, ff).astype(F32)

    gate_w_grad, up_w_grad = unpack(w1_grad[:, :, :half]), unpack(w1_grad[:, :, half:])
    _, norm_one_back = jax.vjp(lambda v: rms_scale(v, gain_one), inputs)
    (input_part,) = norm_one_back(normed_one_grad)
    grad_tokens = (hidden_grad + input_part).astype(BF)
    qkv_w = dot_rows(normed_one, qkv_grad).astype(BF)
    qkv_w = qkv_w.reshape(n_dp, n_ex, wrows, 3 * cols).transpose(1, 0, 2, 3)
    qkv_w = swap(qkv_w, "expert").astype(F32).sum(axis=0).astype(BF)
    qkv_w = swap(qkv_w, "dp").reshape(n_dp, wrows, 3, cols).transpose(2, 1, 0, 3)
    qkv_w = qkv_w.reshape(3, wrows, width).astype(F32)

    small = jnp.concatenate(
        [
            norm_one_grad.reshape(n_all, -1),
            norm_two_grad.reshape(n_all, -1),
            query_gain_grad.reshape(n_all, -1),
            key_gain_grad.reshape(n_all, -1),
            router_grad.reshape(n_all, -1),
        ],
        axis=1,
    )
    small = jnp.sum(swap(small, BOTH).reshape(n_all, -1), axis=0)
    return (
        block_out,
        grad_tokens,
        small[:gw],
        qkv_w[0],
        qkv_w[1],
        qkv_w[2],
        output_grad,
        small[2 * gw : 2 * gw + hw],
        small[2 * gw + hw : 2 * gw + 2 * hw],
        small[gw : 2 * gw],
        small[2 * gw + 2 * hw :].reshape(wrows, expert_total),
        gate_w_grad,
        up_w_grad,
        down_grad,
    )


def solution(mesh):
    rows2 = P(("dp", "expert"), None)
    rows1 = P(("dp", "expert"))
    experts = P("expert", "dp", None)
    return jax.shard_map(
        on_device,
        mesh=mesh,
        in_specs=(rows2, rows2, P(), P(), rows2, rows1, rows2, rows2, rows2, rows2)
        + (rows1, rows1, rows1, rows2, experts, experts, experts),
        out_specs=(rows2, rows2, rows1, rows2, rows2, rows2, rows2)
        + (rows1, rows1, rows1, rows2, experts, experts, experts),
        check_vma=False,
    )
```

```python
from functools import partial
import math

import jax
import jax.numpy as jnp
from jax import lax
from jax.experimental import pallas as pl
from jax.experimental.pallas import tpu as pltpu
from jax.sharding import PartitionSpec as P


HD = 128

norm_eps = 1e-06
rope_base = 10000.0
BF = jnp.bfloat16
F32 = jnp.float32


def rms_scale(features, gain_vec):
    return (
        features
        * lax.rsqrt(jnp.mean(features * features, axis=-1, keepdims=True) + norm_eps)
        * gain_vec
    )


def rotary(features, angles):
    half_dim = features.shape[-1] // 2
    cosine = jnp.cos(angles)[:, None, :]
    sine_part = jnp.sin(angles)[:, None, :]
    front_half = features[..., :half_dim]
    back_half = features[..., half_dim:]
    return jnp.concatenate(
        [front_half * cosine - back_half * sine_part, back_half * cosine + front_half * sine_part],
        axis=-1,
    )


def head_piece(angles, flat_vals, gain_vec):
    count = flat_vals.shape[0]
    shaped = flat_vals.reshape(count, -1, HD)
    return rotary(rms_scale(shaped, gain_vec), angles)


def dot(left_mat, right_mat):
    return jnp.dot(left_mat, right_mat, preferred_element_type=F32)


def dot_rows(left_mat, right_mat):
    return lax.dot_general(
        left_mat, right_mat, (((0,), (0,)), ((), ())), preferred_element_type=F32
    )


def dot_t(left_mat, right_mat):
    return lax.dot_general(
        left_mat, right_mat, (((1,), (1,)), ((), ())), preferred_element_type=F32
    )


BOTH = ("dp", "expert")


def swap(blocks, axes):
    return lax.all_to_all(blocks, axes, split_axis=0, concat_axis=0, tiled=True)


def gather(shard, axes):
    return lax.all_gather(shard, axes, axis=0, tiled=True)


def scatter(partial_sum, axes):
    return lax.psum_scatter(partial_sum, axes, scatter_dimension=0, tiled=True)


def ring_order(size):
    return list(range(0, size, 2)) + list(range(1, size, 2))[::-1]


def ring_perm(n_dp, steps):
    order = ring_order(n_dp // 2)
    size = len(order)
    pairs = []
    for spot in range(size):
        for inner in range(2):
            target = order[(spot + steps) % size]
            pairs.append((order[spot] * 2 + inner, target * 2 + inner))
    return pairs


def ring_shift(vals, steps):
    return lax.ppermute(vals, "dp", ring_perm(lax.axis_size("dp"), steps))


def flip(vals, axis, bit):
    size = lax.axis_size(axis)
    return lax.ppermute(vals, axis, [(i, i ^ bit) for i in range(size)])


def core_flip(vals):
    return flip(vals, "expert", 1)


def cross(vals, inner, bits):
    if inner == 0:
        return flip(vals, "expert", bits)
    if bits == 0:
        return flip(vals, "dp", 1)
    n_ex = lax.axis_size("expert")
    size = lax.axis_size("dp") * n_ex
    pairs = [(i, ((i // n_ex) ^ 1) * n_ex + ((i % n_ex) ^ bits)) for i in range(size)]
    return lax.ppermute(vals, BOTH, pairs)


def peers():
    size = lax.axis_size("expert")
    return [(inner, bits) for bits in range(0, size, 2) for inner in range(2)][1:]


def ring_blocks(vals, urgent=False):
    blocks = [vals]
    for step in range(1, lax.axis_size("dp") // 2):
        blocks.append(ring_shift(after(vals, blocks[1]) if urgent and step > 1 else vals, step))
    return blocks


def after(vals, *others):
    return lax.optimization_barrier((vals,) + others)[0]


def pick_rows(vals, index):
    return vals.at[index].get(mode="promise_in_bounds")


def add32(left, right):
    return left.astype(F32) + right.astype(F32)


def add(left, right):
    return (left.astype(F32) + right.astype(F32)).astype(left.dtype)


def x_flip(vals):
    return flip(vals, "expert", 2)


def y_flip(vals):
    return flip(vals, "dp", 1)


def split_at(width):
    return width // 256 * 128


def gather_peers(vals):
    if lax.axis_size("expert") != 4:
        return jnp.stack([vals] + [cross(vals, *peer) for peer in peers()])
    cut = split_at(vals.shape[-1])
    left, right = vals[..., :cut], vals[..., cut:]
    left_y, right_x = y_flip(left), x_flip(right)
    left_pair, right_pair = jnp.stack([left, left_y]), jnp.stack([right, right_x])
    left_far, right_far = x_flip(left_pair), y_flip(right_pair)
    return jnp.stack(
        [
            vals,
            jnp.concatenate([left_y, right_far[0]], axis=-1),
            jnp.concatenate([left_far[0], right_x], axis=-1),
            jnp.concatenate([left_far[1], right_far[1]], axis=-1),
        ]
    )


def reduce_peers(vals):
    if lax.axis_size("expert") == 4:
        cut = split_at(vals.shape[-1])
        own, at_y, at_x, at_xy = vals[0], vals[1], vals[2], vals[3]
        left = x_flip(jnp.stack([at_x[..., :cut], at_xy[..., :cut]]))
        right = y_flip(jnp.stack([at_y[..., cut:], at_xy[..., cut:]]))
        left_y = add(at_y[..., :cut], left[1])
        right_x = add(at_x[..., cut:], right[1])
        left_y, right_x = y_flip(left_y), x_flip(right_x)
        left = add(add32(own[..., :cut], left[0]), left_y).astype(vals.dtype)
        right = add(add32(own[..., cut:], right[0]), right_x).astype(vals.dtype)
        return jnp.concatenate([left, right], axis=-1)
    total = vals[0].astype(F32)
    for spot, peer in enumerate(peers()):
        total = total + cross(vals[spot + 1], *peer).astype(F32)
    return total.astype(vals.dtype)


def walk_tables(n_dp):
    ring = ring_order(n_dp // 2)
    size = len(ring)
    ring_arr = jnp.array(ring, jnp.int32)
    spot_arr = jnp.array([ring.index(i) for i in range(size)], jnp.int32)
    member = lax.axis_index("dp")
    my_spot = spot_arr[member // 2]
    walk = jnp.arange(n_dp, dtype=jnp.int32)
    inner = (member % 2) ^ (walk % 2)
    source = ring_arr[(my_spot - walk // 2) % size] * 2 + inner
    target = ring_arr[(my_spot + walk // 2) % size] * 2 + inner
    step_of = ((my_spot - spot_arr[walk // 2]) % size) * 2 + inner
    return source, target, step_of


def walk_perm(n_dp, index):
    pairs = ring_perm(n_dp, index // 2)
    return [(src, dst ^ (index % 2)) for src, dst in pairs]


def walk_swap(blocks, tables, wait_for=None):
    n_dp = blocks.shape[0]
    _, target, step_of = tables
    moved = []
    for index in range(n_dp):
        block = lax.dynamic_index_in_dim(blocks, target[index], 0, keepdims=False)
        if index:
            block = lax.ppermute(block, "dp", walk_perm(n_dp, index))
        moved.append(block)
    if wait_for is not None:
        moved = [after(block, *wait_for) for block in moved]
    return pick_rows(jnp.stack(moved), step_of)


def home(parts):
    total = parts[0].astype(F32)
    for step in range(1, len(parts)):
        total = total + ring_shift(parts[step], -step).astype(F32)
    return total


def expert_kernel(halves, width, xa, xb, ya, yb, w1, w1t, w2, w2t, pick, place, outs):
    ma, mb, ra, rb, pre_out, inner_out = outs
    step = pl.program_id(0)
    first = step < halves
    x_all = jnp.where(first, xa[...], xb[...])
    dy = jnp.where(first, ya[...], yb[...]).reshape(x_all.shape[0], width)
    x = x_all[:, :width]
    half = w2.shape[0]
    gates = dot(x_all[:, width:], pick[...])
    pre = dot(x, w1[...])
    gate_val, up_val = pre[:, :half], pre[:, half:]
    sig = 1.0 / (1.0 + jnp.exp(-gate_val))
    silu = gate_val * sig
    inner = (silu * up_val).astype(BF).astype(F32)
    gated = (gates * inner).astype(BF)
    inner_out[...] = gated
    mix = dot(gated, w2[...]).astype(BF)
    back = dot(dy, w2t[...])
    prod = inner * back
    prod_hi = prod.astype(BF)
    prod_lo = (prod - prod_hi.astype(F32)).astype(BF)
    gate_grad = (dot(prod_hi, place[...]) + dot(prod_lo, place[...])).astype(BF)
    inner_grad = gates * back
    gate_pre = (inner_grad * up_val * sig * (1.0 + gate_val * (1.0 - sig))).astype(BF)
    up_pre = (inner_grad * silu).astype(BF)
    pre_out[:, :half] = gate_pre
    pre_out[:, half:] = up_pre
    rows = (dot(gate_pre, w1t[:half, :]) + dot(up_pre, w1t[half:, :])).astype(BF)

    @pl.when(first)
    def _():
        ma[...] = mix
        ra[:, :width] = rows
        ra[:, width:] = gate_grad

    @pl.when(jnp.logical_not(first))
    def _():
        mb[...] = mix
        rb[:, :width] = rows
        rb[:, width:] = gate_grad


def experts(chunk, xa, xb, ya, yb, w1, w1t, w2, w2t, pick, place):
    count, wide = xa.shape
    rows, width = ya.shape[2:]
    half = w2.shape[0]
    tile = 2 * rows
    halves = count // tile
    front = lambda i: (jnp.minimum(i, halves - 1), 0)
    rear = lambda i: (jnp.maximum(i - halves, 0), 0)
    whole = lambda arr: pl.BlockSpec(arr.shape, lambda i: (0, 0), pipeline_mode=pl.Buffered(1))
    back_wide = width + place.shape[1]

    def body(xa, xb, ya, yb, w1, w1t, w2, w2t, pick, place, *outs):
        expert_kernel(halves, width, xa, xb, ya, yb, w1, w1t, w2, w2t, pick, place, outs)

    flops = 2 * 2 * count * width * half * 6
    return pl.pallas_call(
        body,
        grid=(2 * halves,),
        in_specs=[
            pl.BlockSpec((tile, wide), front),
            pl.BlockSpec((tile, wide), rear),
            pl.BlockSpec((2, None, rows, width), lambda i: (front(i)[0], chunk, 0, 0)),
            pl.BlockSpec((2, None, rows, width), lambda i: (rear(i)[0], chunk, 0, 0)),
        ]
        + [whole(arr) for arr in (w1, w1t, w2, w2t, pick, place)],
        out_specs=[
            pl.BlockSpec((tile, width), front),
            pl.BlockSpec((tile, width), rear),
            pl.BlockSpec((tile, back_wide), front),
            pl.BlockSpec((tile, back_wide), rear),
            pl.BlockSpec((tile, 2 * half), lambda i: (i, 0)),
            pl.BlockSpec((tile, half), lambda i: (i, 0)),
        ],
        out_shape=[
            jax.ShapeDtypeStruct((count, width), BF),
            jax.ShapeDtypeStruct((count, width), BF),
            jax.ShapeDtypeStruct((count, back_wide), BF),
            jax.ShapeDtypeStruct((count, back_wide), BF),
            jax.ShapeDtypeStruct((2 * count, 2 * half), BF),
            jax.ShapeDtypeStruct((2 * count, half), BF),
        ],
        cost_estimate=pl.CostEstimate(
            flops=flops, transcendentals=2 * count * half, bytes_accessed=20 * count * width
        ),
        name="experts",
    )(xa, xb, ya, yb, w1, w1t, w2, w2t, pick, place)


def attend_kernel(scale, q, k, v, bias, out):
    scores = dot_t(q[...], k[...]) * scale + bias[...]
    weights = jnp.exp(scores - jnp.max(scores, axis=-1, keepdims=True))
    probs = (weights / jnp.sum(weights, axis=-1, keepdims=True)).astype(BF)
    out[...] = dot(probs, v[...]).astype(BF)


def attend(q, k, v, bias, scale):
    count, cols = q.shape
    tile = min(256, count)
    mine = pl.BlockSpec((tile, HD), lambda h, i: (i, h))
    full = pl.BlockSpec((count, HD), lambda h, i: (0, h))
    return pl.pallas_call(
        partial(attend_kernel, scale),
        grid=(cols // HD, count // tile),
        in_specs=[mine, full, full, pl.BlockSpec((1, count), lambda h, i: (0, 0))],
        out_specs=mine,
        out_shape=jax.ShapeDtypeStruct((count, cols), BF),
        cost_estimate=pl.CostEstimate(
            flops=4 * count * count * cols,
            transcendentals=count * count * cols // HD,
            bytes_accessed=8 * count * cols,
        ),
        name="attend",
    )(q, k, v, bias)


def attend_back_kernel(scale, q, k, v, bias, grad, dq, dk, dv, dk_sum, dv_sum):
    step = pl.program_id(1)
    scores = dot_t(q[...], k[...]) * scale + bias[...]
    weights = jnp.exp(scores - jnp.max(scores, axis=-1, keepdims=True))
    probs = weights / jnp.sum(weights, axis=-1, keepdims=True)
    prob_grad = dot_t(grad[...], v[...])
    mean = jnp.sum(probs * prob_grad, axis=-1, keepdims=True)
    score_grad = (probs * (prob_grad - mean)).astype(BF)
    dq[...] = dot(score_grad, k[...]) * scale
    dk_part = dot_rows(score_grad, q[...]) * scale
    dv_part = dot_rows(probs.astype(BF), grad[...])

    @pl.when(step == 0)
    def _():
        dk_sum[...] = dk_part
        dv_sum[...] = dv_part

    @pl.when(step > 0)
    def _():
        dk_sum[...] += dk_part
        dv_sum[...] += dv_part

    @pl.when(step == pl.num_programs(1) - 1)
    def _():
        dk[...] = dk_sum[...]
        dv[...] = dv_sum[...].astype(BF)


def attend_back(q, k, v, bias, grad, scale):
    count, cols = q.shape
    tile = min(256, count)
    mine = pl.BlockSpec((tile, HD), lambda h, i: (i, h))
    full = pl.BlockSpec((count, HD), lambda h, i: (0, h))
    return pl.pallas_call(
        partial(attend_back_kernel, scale),
        grid=(cols // HD, count // tile),
        in_specs=[mine, full, full, pl.BlockSpec((1, count), lambda h, i: (0, 0)), mine],
        out_specs=[mine, full, full],
        out_shape=[
            jax.ShapeDtypeStruct((count, cols), F32),
            jax.ShapeDtypeStruct((count, cols), F32),
            jax.ShapeDtypeStruct((count, cols), BF),
        ],
        scratch_shapes=[pltpu.VMEM((count, HD), F32), pltpu.VMEM((count, HD), F32)],
        cost_estimate=pl.CostEstimate(
            flops=10 * count * count * cols,
            transcendentals=count * count * cols // HD,
            bytes_accessed=20 * count * cols,
        ),
        name="attend_back",
    )(q, k, v, bias, grad)


def lanes(count):
    return -(-count // 128) * 128


def on_device(
    tokens,
    cotangent,
    lengths,
    piece_order,
    routes,
    attn_gain,
    w_query,
    w_key,
    w_value,
    w_output,
    query_gain,
    key_gain,
    moe_gain,
    w_router,
    w_gate,
    w_up,
    w_down,
):
    rows, width = tokens.shape
    seq_id = lax.axis_index("expert")
    n_dp = lax.axis_size("dp")
    n_ex = lax.axis_size("expert")
    n_all = n_dp * n_ex
    local_count, _, ff = w_gate.shape
    expert_total = local_count * n_ex
    ff_part = ff // n_dp
    cols = width // n_dp
    wrows = w_query.shape[0]
    score_scale = 1.0 / math.sqrt(HD)

    seq_tokens = gather(tokens, "dp")
    member = lax.axis_index("dp")
    tables = walk_tables(n_dp)
    member_of_walk = tables[0]
    qkv = jnp.stack([w_query, w_key, w_value]).astype(BF).reshape(3, wrows, n_dp, cols)
    qkv = swap(qkv.transpose(2, 1, 0, 3), "dp")
    gains = jnp.concatenate(
        [attn_gain, moe_gain, query_gain, key_gain, w_router.T.reshape(-1)]
    )
    gains = after(gains, qkv)
    gains_all = swap(jnp.broadcast_to(gains, (n_all, gains.shape[0])), BOTH)
    gw, hw = attn_gain.shape[0], query_gain.shape[0]
    gain_one = gains_all[:, :gw].reshape(-1)
    gain_two = gains_all[:, gw : 2 * gw].reshape(-1)
    gain_q = gains_all[:, 2 * gw : 2 * gw + hw].reshape(-1)
    gain_k = gains_all[:, 2 * gw + hw : 2 * gw + 2 * hw].reshape(-1)
    wr_all = gains_all[:, 2 * gw + 2 * hw :].reshape(n_all, expert_total, wrows)
    wr_all = wr_all.transpose(1, 0, 2).reshape(expert_total, width).astype(BF)

    qkv = qkv.reshape(1, n_dp, wrows, 3 * cols)
    bit = 1
    while bit < n_ex:
        qkv = jnp.concatenate([qkv, flip(qkv, "expert", bit)], axis=0)
        bit *= 2
    qkv = pick_rows(qkv, seq_id ^ jnp.arange(n_ex, dtype=jnp.int32))
    qkv = qkv.transpose(1, 0, 2, 3).reshape(width, 3 * cols)
    wo_all = gather(w_output.astype(BF), BOTH)
    w1 = jnp.stack([w_gate, w_up]).astype(BF).reshape(2, local_count, cols, n_dp, ff_part)
    w1 = w1.transpose(3, 2, 0, 1, 4).reshape(n_dp, cols, -1)
    w1 = after(w1, gains_all)
    dy_ring = jnp.stack(ring_blocks(after(cotangent, gains_all)))
    w2 = w_down.astype(BF).reshape(local_count * ff_part, width)
    half = local_count * ff_part

    seq_in = seq_tokens.astype(F32)
    normed_one = rms_scale(seq_in, gain_one).astype(BF)
    qkv_flat = dot(normed_one, qkv)
    offsets = jnp.arange(rows, dtype=jnp.int32)
    position = (piece_order[seq_id][:, None] * rows + offsets[None, :]).reshape(-1)
    visible = position < lengths[seq_id]
    half_dim = HD // 2
    frequency = rope_base ** (-(jnp.arange(half_dim, dtype=F32) * 2.0 / HD))
    angles = position.astype(F32)[:, None] * frequency[None, :]
    query_rot, query_back = jax.vjp(partial(head_piece, angles), qkv_flat[:, :cols], gain_q)
    key_rot, key_back = jax.vjp(partial(head_piece, angles), qkv_flat[:, cols : 2 * cols], gain_k)
    query_bf = query_rot.astype(BF).reshape(-1, cols)
    key_bf = key_rot.astype(BF).reshape(-1, cols)
    value_bf = qkv_flat[:, 2 * cols :].astype(BF)
    bias = jnp.where(visible, 0.0, -jnp.inf).astype(F32)[None, :]
    attended = attend(query_bf, key_bf, value_bf, bias, score_scale)
    attended = swap(attended.reshape(n_dp, rows, cols), "dp")
    dy_near = gather_peers(after(dy_ring, attended))
    dy_far = core_flip(dy_near)
    attended = attended.transpose(1, 0, 2).reshape(rows, width)

    inputs = tokens.astype(F32)
    hidden_one = inputs + dot(attended, wo_all)
    normed_two = rms_scale(hidden_one, gain_two).astype(BF)
    router_logits = dot_t(normed_two, wr_all)
    expert_ids = jnp.arange(expert_total, dtype=jnp.int32)
    routed = jnp.any(routes[:, :, None] == expert_ids[None, None, :], axis=1)
    masked_logits = jnp.where(routed, router_logits, -jnp.inf)
    gates = jax.nn.softmax(masked_logits, axis=-1)
    gates_hi = gates.astype(BF)
    gates_lo = (gates - gates_hi.astype(F32)).astype(BF)
    spare = lanes(2 * expert_total) - 2 * expert_total
    payload = jnp.concatenate(
        [normed_two, gates_hi, gates_lo, jnp.zeros((rows, spare), BF)], axis=1
    )
    w1 = walk_swap(w1, tables, (payload,))
    w1 = w1.reshape(width, -1)
    w1t, w2t = w1.T, w2.T
    unit = jnp.arange(half, dtype=jnp.int32) // ff_part + seq_id * local_count
    gate_col = jnp.arange(lanes(2 * expert_total), dtype=jnp.int32)
    pick = (
        (gate_col[:, None] == unit[None, :]) | (gate_col[:, None] == unit[None, :] + expert_total)
    ).astype(BF)
    grad_col = jnp.arange(lanes(expert_total * n_dp), dtype=jnp.int32)
    place = (grad_col[None, :] == (unit * n_dp + member)[:, None]).astype(BF)

    lean = n_all * rows > 4096
    n2_sets, mix_parts, home_parts, pre_grads, gated_inners = [], [], [], [], []
    w1_grad, down_grad = 0.0, 0.0
    for step, block in enumerate(ring_blocks(payload, True)):
        near = gather_peers(block).reshape(-1, block.shape[-1])
        far = core_flip(near)
        ma, mb, ra, rb, pre_grad, gated_inner = experts(
            step, near, far, dy_near, dy_far, w1, w1t, w2, w2t, pick, place
        )
        part = add(ra, core_flip(rb)).reshape(-1, rows, ra.shape[1])
        home_parts.append(reduce_peers(part))
        if lean:
            mix_parts.append(reduce_peers(add(ma, core_flip(mb)).reshape(-1, rows, width)))
            cut = pre_grad.shape[0] // 2
            w1_grad = w1_grad + dot_rows(near[:, :width], pre_grad[:cut])
            w1_grad = w1_grad + dot_rows(far[:, :width], pre_grad[cut:])
            down_grad = down_grad + dot_rows(gated_inner[:cut], dy_near[:, step].reshape(-1, width))
            down_grad = down_grad + dot_rows(gated_inner[cut:], dy_far[:, step].reshape(-1, width))
            w1_grad, down_grad, dy_near, dy_far, mix_parts, home_parts, payload = (
                lax.optimization_barrier(
                    (w1_grad, down_grad, dy_near, dy_far, mix_parts, home_parts, payload)
                )
            )
        else:
            n2_sets += [near, far]
            mix_parts.append((ma, mb))
            pre_grads.append(pre_grad)
            gated_inners.append(gated_inner)
    returned = home(home_parts)
    if not lean:
        mix_near = jnp.stack([m[0].reshape(-1, rows, width) for m in mix_parts], axis=1)
        mix_far = jnp.stack([m[1].reshape(-1, rows, width) for m in mix_parts], axis=1)
        mix_far = after(mix_far, returned)
        mix_near = add(mix_near, core_flip(mix_far))
        mix_parts = list(reduce_peers(mix_near))
        by_chunk = jnp.stack([g.reshape(2, -1, rows, half) for g in gated_inners], axis=2)
        by_chunk = by_chunk.reshape(2, -1, half)
        down_grad = dot_rows(by_chunk[0], dy_near.reshape(-1, width)) + dot_rows(
            by_chunk[1], dy_far.reshape(-1, width)
        )
        n2_all = jnp.concatenate([part[:, :width] for part in n2_sets], axis=0)
        pre_all = jnp.concatenate(pre_grads, axis=0)
        w1_grad = dot_rows(n2_all, pre_all)
    w1_grad = w1_grad.astype(BF)
    if not lean:
        w1_grad = after(w1_grad, part)
    token_grads = returned[:, :width]
    gg = returned[:, width : width + expert_total * n_dp].reshape(rows, expert_total, n_dp)
    gg = jnp.sum(gg, axis=-1)
    mixed = home(mix_parts)
    down_grad = down_grad.reshape(local_count, ff_part, width)
    weighted = gates * gg
    logit_bf = (weighted - gates * jnp.sum(weighted, axis=-1, keepdims=True)).astype(BF)
    router_grad = dot_rows(normed_two, logit_bf)
    normed_two_grad = token_grads + dot(logit_bf, wr_all)
    _, norm_two_back = jax.vjp(rms_scale, hidden_one, gain_two)
    hidden_part, norm_two_grad = norm_two_back(normed_two_grad)
    hidden_grad = cotangent.astype(F32) + hidden_part
    attn_grad_bf = hidden_grad.astype(BF)
    output_grad = scatter(dot_rows(attended, attn_grad_bf).astype(BF), BOTH).astype(F32)
    attended_grad = dot_t(attn_grad_bf, wo_all).astype(BF)
    attended_grad = swap(attended_grad.reshape(rows, n_dp, cols).transpose(1, 0, 2), "dp")
    attended_grad = attended_grad.reshape(-1, cols)

    query_grad, key_grad, value_grad = attend_back(
        query_bf, key_bf, value_bf, bias, attended_grad, score_scale
    )
    block_out = (after(hidden_one, query_grad) + mixed).astype(BF)
    query_grad = query_grad.reshape(-1, cols // HD, HD)
    key_grad = key_grad.reshape(-1, cols // HD, HD)
    query_flat_grad, query_gain_grad = query_back(query_grad)
    key_flat_grad, key_gain_grad = key_back(key_grad)
    qkv_grad = jnp.concatenate(
        [query_flat_grad.astype(BF), key_flat_grad.astype(BF), value_grad],
        axis=1,
    )
    walk_grad = pick_rows(qkv_grad.reshape(n_dp, rows, 3 * cols), member_of_walk)
    part_grad = dot_t(walk_grad.reshape(-1, 3 * cols), qkv)
    walk_in = pick_rows(seq_tokens.reshape(n_dp, rows, width), member_of_walk)
    seq_in = walk_in.reshape(-1, width).astype(F32)
    seq_scale = lax.rsqrt(jnp.mean(seq_in * seq_in, axis=-1, keepdims=True) + norm_eps)
    norm_one_grad = jnp.sum(part_grad * (seq_in * seq_scale), axis=0)
    part_bf = part_grad.astype(BF).reshape(n_dp // 2, 2, rows, width)
    sums = []
    for step in range(n_dp // 2):
        sums.append(add(part_bf[step, 0], flip(part_bf[step, 1], "dp", 1)))
    normed_one_grad = home(sums)
    w1_grad = walk_swap(w1_grad.reshape(n_dp, cols, -1), tables, (sums[-1], mix_parts[-1]))

    def unpack(blocks):
        blocks = blocks.reshape(n_dp, cols, local_count, ff_part).transpose(2, 1, 0, 3)
        return blocks.reshape(local_count, cols, ff).astype(F32)

    gate_w_grad, up_w_grad = unpack(w1_grad[:, :, :half]), unpack(w1_grad[:, :, half:])
    _, norm_one_back = jax.vjp(lambda v: rms_scale(v, gain_one), inputs)
    (input_part,) = norm_one_back(normed_one_grad)
    grad_tokens = (hidden_grad + input_part).astype(BF)
    qkv_w = dot_rows(normed_one, qkv_grad).astype(BF)
    qkv_w = qkv_w.reshape(n_dp, n_ex, wrows, 3 * cols).transpose(1, 0, 2, 3)
    qkv_w = swap(qkv_w, "expert").astype(F32).sum(axis=0).astype(BF)
    qkv_w = swap(qkv_w, "dp").reshape(n_dp, wrows, 3, cols).transpose(2, 1, 0, 3)
    qkv_w = qkv_w.reshape(3, wrows, width).astype(F32)

    small = jnp.concatenate(
        [
            norm_one_grad.reshape(n_all, -1),
            norm_two_grad.reshape(n_all, -1),
            query_gain_grad.reshape(n_all, -1),
            key_gain_grad.reshape(n_all, -1),
            router_grad.reshape(n_all, -1),
        ],
        axis=1,
    )
    small = jnp.sum(swap(small, BOTH).reshape(n_all, -1), axis=0)
    return (
        block_out,
        grad_tokens,
        small[:gw],
        qkv_w[0],
        qkv_w[1],
        qkv_w[2],
        output_grad,
        small[2 * gw : 2 * gw + hw],
        small[2 * gw + hw : 2 * gw + 2 * hw],
        small[gw : 2 * gw],
        small[2 * gw + 2 * hw :].reshape(wrows, expert_total),
        gate_w_grad,
        up_w_grad,
        down_grad,
    )


def solution(mesh):
    rows2 = P(("dp", "expert"), None)
    rows1 = P(("dp", "expert"))
    experts = P("expert", "dp", None)
    return jax.shard_map(
        on_device,
        mesh=mesh,
        in_specs=(rows2, rows2, P(), P(), rows2, rows1, rows2, rows2, rows2, rows2)
        + (rows1, rows1, rows1, rows2, experts, experts, experts),
        out_specs=(rows2, rows2, rows1, rows2, rows2, rows2, rows2)
        + (rows1, rows1, rows1, rows2, experts, experts, experts),
        check_vma=False,
    )
```
